32 devices in a mesh: groups: 2 (over y), store: 4 (over z), head: 2 (over x), sub: 2 (over core).
Axes of the slice: x: 2, y: 2, z: 4, core: 2. Of those that a mesh axis runs over, the one named last changes fastest.
Arguments:
- fresh_query: bfloat16 [16, 528, 8192], P(('groups', 'store'), None, ('head', 'sub')), parts along dimension 0, may hold values from -20 to 20
- fresh_keys: bfloat16 [16, 528, 1024], P(('groups', 'store'), None, 'head'), parts along dimension 0, may hold values from -6 to 6
- fresh_values: bfloat16 [16, 528, 1024], P(('groups', 'store'), None, 'head'), parts along dimension 0, may hold values from -24 to 24
- store_keys: bfloat16 [64, 512, 1024], P(('groups', 'store'), 'sub', 'head'), parts along dimension 0, may hold values from -6 to 6
- store_values: bfloat16 [64, 512, 1024], P(('groups', 'store'), 'sub', 'head'), parts along dimension 0, may hold values from -24 to 24
- span_ids: int32 [16, 6], P('groups'), parts along dimension 0, may hold values from 0 to 31, as said below
- span_slot: int32 [64], P('groups'), parts along dimension 0, may hold values from 0 to 31, as said below
- select_pos: int32 [16, 464], P('groups'), parts along dimension 0, may hold values from 0 to 3071, as said below
- ask_len: int32 [16], P('groups'), parts along dimension 0, may hold values from 1 to 64, as said below
Outputs:
- attn_out: bfloat16 [16, 528, 8192], P(('groups', 'store'), None, ('head', 'sub')), parts along dimension 0
The draws below stay inside these ranges and needn't reach their ends.
There are 2 independent parts, one for each index of `groups`. The reference program is written for one: setup_inputs(seed, part) draws one part's arguments, and reference() takes and returns one part's arrays. A program takes and returns all parts, laid end to end along the dimension named above; each array names one. Nothing has to cross between parts.
Inputs may be any that keep to these rules, and one draw needn't show every extreme that they name: `span_ids`: the 6 spans of a request are distinct. Over the 2 requests of one store index (requests s * 2 to s * 2 + 1) all named spans are distinct, and at most 3 of them have slots on any one store index, exactly 3 on some. `span_slot`: A permutation; the span with slot v is held by store index v // 8. `select_pos`: strictly increasing within each request. `ask_len`: some request has 64.
All inputs are finite; a program needn't handle non-finite values.
Results may differ from the reference program's by a relative error of at most 0.0045.
Values may be sent and summed in bfloat16 or wider, within the bound.
No kernel may reach another device: no remote copies, remote signals or barrier semaphores. Data moves between devices by JAX's collectives and lax.ppermute only.
A program may use at most 128 MiB of HBM per device.

```python
import jax
import jax.numpy as jnp
from jax import lax

HD = 128
QH = 64
KVH = 8
GROUP = 8
SPAN = 512
NCH = 6
CTX = 3072
SEL = 464
QLEN = 64
ROWS = 528
REQ_DEV = 2
CH_DEV = 8
REQS = 8
NCHUNKS = 32
N_STORE = 4


def span_layout(key):
    key_perm, key_owner, key_base = jax.random.split(jax.random.fold_in(key, 7), 3)
    slot_of = jax.random.permutation(key_perm, NCHUNKS).astype(jnp.int32)
    span_at = jnp.argsort(slot_of).astype(jnp.int32)
    references = REQ_DEV * NCH
    owner_scores = jax.random.randint(key_owner, (N_STORE, N_STORE), 0, 1 << 20) * N_STORE + jnp.arange(N_STORE)[None, :]
    owner_order = jnp.argsort(owner_scores, axis=1).astype(jnp.int32)
    base_picks = jax.random.randint(key_base, (3, N_STORE, N_STORE), 0, CH_DEV)
    base_place = jnp.min(base_picks, axis=0)
    counter = jnp.arange(references)
    owners = owner_order[:, counter % N_STORE]
    turns = counter // N_STORE
    starts = jnp.take_along_axis(base_place, owners, axis=1)
    slot_ids = owners * CH_DEV + (starts + turns[None, :]) % CH_DEV
    span_names = span_at[slot_ids].reshape(N_STORE * REQ_DEV, NCH)
    return (span_names.astype(jnp.int32), slot_of)


def draw_span_ids(key, part):
    return span_layout(key)[0]


def draw_span_slot(key, part):
    return span_layout(key)[1]


def draw_select_pos(key, part):
    scores = jax.random.randint(jax.random.fold_in(key, 11), (REQS, CTX), 0, 1 << 18) * CTX + jnp.arange(CTX)[None, :]
    picked = jnp.argsort(scores, axis=1)[:, :SEL]
    return jnp.sort(picked, axis=1).astype(jnp.int32)


def draw_ask_len(key, part):
    key_len, key_spot = jax.random.split(jax.random.fold_in(key, 13))
    lengths = jax.random.randint(key_len, (REQS,), 1, QLEN + 1)
    spot = jax.random.randint(key_spot, (), 0, REQS)
    return jnp.where(jnp.arange(REQS) == spot, QLEN, lengths).astype(jnp.int32)


def drawn_rows(key):
    parts_keys = jax.random.split(jax.random.fold_in(key, 17), 2)
    row_keys = jax.random.truncated_normal(parts_keys[0], -6.0, 6.0, (REQS, ROWS, KVH * HD), jnp.float32)
    row_query = jax.random.truncated_normal(parts_keys[1], -6.0, 6.0, (REQS, ROWS, QH * HD), jnp.float32)
    return (row_keys, row_query)


def draw_fresh_keys(key, part):
    return drawn_rows(key)[0].astype(jnp.bfloat16)


def draw_fresh_query(key, part):
    return drawn_rows(key)[1].astype(jnp.bfloat16)


def levels(key, dims, cuts, low, largest):
    def one(axis_at, shards_of):
        draws = jax.random.uniform(jax.random.fold_in(jax.random.fold_in(key, 6), axis_at), (shards_of,), jnp.float32, low / len(cuts), largest / len(cuts))
        return jnp.repeat(jnp.exp(draws), dims[axis_at] // shards_of).reshape((-1,) + (1,) * (len(dims) - axis_at - 1))

    loudness = one(*cuts[0])
    for cut in cuts[1:]:
        loudness = loudness * one(*cut)
    return loudness


def scatter_about(key, dims, deviation, reach, shards=(), kind=jnp.bfloat16):
    result = jax.random.normal(key, dims, jnp.float32) * deviation
    if len(shards) > 0:
        result = levels(key, dims, shards, -0.22, 0.18) * result
    return jnp.clip(result, min=-reach, max=reach).astype(kind)


def setup_inputs(seed: int = 0, part: int = 0) -> dict:
    keys = jax.random.split(jax.random.key(seed), 10)
    own_keys = jax.random.split(jax.random.fold_in(keys[9], part), 10)
    return {
        "fresh_query": draw_fresh_query(jax.random.fold_in(jax.random.fold_in(keys[9], part), 71), part),
        "fresh_keys": draw_fresh_keys(jax.random.fold_in(jax.random.fold_in(keys[9], part), 71), part),
        "fresh_values": scatter_about(own_keys[2], (REQS, ROWS, KVH * HD), 4.0, 24.0, ((0, 4), (2, 2))),
        "store_keys": scatter_about(own_keys[3], (NCHUNKS, SPAN, KVH * HD), 1.0, 6.0, ((0, 4), (1, 2), (2, 2))),
        "store_values": scatter_about(own_keys[4], (NCHUNKS, SPAN, KVH * HD), 4.0, 24.0, ((0, 4), (1, 2), (2, 2))),
        "span_ids": draw_span_ids(jax.random.fold_in(jax.random.fold_in(keys[9], part), 71), part),
        "span_slot": draw_span_slot(jax.random.fold_in(jax.random.fold_in(keys[9], part), 71), part),
        "select_pos": draw_select_pos(jax.random.fold_in(jax.random.fold_in(keys[9], part), 71), part),
        "ask_len": draw_ask_len(jax.random.fold_in(jax.random.fold_in(keys[9], part), 71), part),
    }


NEGATIVE = -1.0e30


def reference(fresh_query, fresh_keys, fresh_values, store_keys, store_values, span_ids, span_slot, select_pos, ask_len):
    slot_ids = span_slot[span_ids]
    score_scale = HD ** -0.5

    def per_request(pieces):
        query_rows, key_rows, value_rows, request_slots, positions, ask_length = pieces
        context_keys = store_keys[request_slots].reshape(CTX, KVH * HD)
        context_values = store_values[request_slots].reshape(CTX, KVH * HD)
        context_keys = context_keys.at[positions].set(key_rows[:SEL])
        context_values = context_values.at[positions].set(value_rows[:SEL])
        all_keys = jnp.concatenate([context_keys, key_rows[SEL:]], axis=0)
        all_values = jnp.concatenate([context_values, value_rows[SEL:]], axis=0)
        query_pos = jnp.concatenate([positions, CTX + jnp.arange(QLEN, dtype=jnp.int32)])
        key_pos = jnp.arange(CTX + QLEN, dtype=jnp.int32)
        key_live = key_pos < CTX + ask_length
        allowed = (key_pos[None, :] <= query_pos[:, None]) & key_live[None, :]
        row_live = jnp.arange(ROWS, dtype=jnp.int32) < SEL + ask_length

        def per_head(kv_head):
            head_keys = lax.dynamic_slice_in_dim(all_keys, kv_head * HD, HD, 1).astype(jnp.float32)
            head_values = lax.dynamic_slice_in_dim(all_values, kv_head * HD, HD, 1).astype(jnp.float32)
            head_query = lax.dynamic_slice_in_dim(query_rows, kv_head * GROUP * HD, GROUP * HD, 1)
            head_query = head_query.astype(jnp.float32).reshape(ROWS, GROUP, HD)
            scores = jnp.einsum("rgd,kd->grk", head_query, head_keys) * score_scale
            scores = jnp.where(allowed[None], scores, NEGATIVE)
            row_max = jnp.max(scores, axis=-1, keepdims=True)
            powers = jnp.where(allowed[None], jnp.exp(scores - row_max), 0.0)
            totals = jnp.sum(powers, axis=-1)
            weights = lax.optimization_barrier(powers.astype(jnp.bfloat16)).astype(jnp.float32)
            mixed = jnp.einsum("grk,kd->rgd", weights, head_values)
            return mixed / jnp.transpose(totals)[:, :, None]

        heads_out = lax.map(per_head, jnp.arange(KVH, dtype=jnp.int32))
        merged = jnp.transpose(heads_out, (1, 0, 2, 3)).reshape(ROWS, QH * HD)
        return jnp.where(row_live[:, None], merged, 0.0).astype(jnp.bfloat16)

    return lax.map(per_request, (fresh_query, fresh_keys, fresh_values, slot_ids, select_pos, ask_len))
```

```python
import functools
import math

import jax
import jax.numpy as jnp
from jax import lax
from jax.experimental import pallas as pl
from jax.experimental.pallas import tpu as pltpu
from jax.sharding import PartitionSpec as P

HD = 128
GROUP = 8
SPAN = 512
NCH = 6
CTX = 3072
SEL = 464
QLEN = 64
ROWS = 528

NEGATIVE = -1e30
FAR = 1 << 28
TILE = 176
LOG_SCALE = HD ** (-0.5) * math.log2(math.e)


class Plan:
    def __init__(self, fresh_query, fresh_keys, store_keys, span_ids, span_slot):
        self.stores = lax.axis_size("store")
        self.cores = lax.axis_size("sub")
        self.req_dev = fresh_query.shape[0]
        self.ch_dev, self.half, self.kv_columns = store_keys.shape
        self.refs = self.req_dev * NCH
        self.capacity = (self.refs + self.stores - 1) // self.stores
        self.q_columns = fresh_query.shape[2]
        self.q_heads = self.q_columns // HD
        self.kv_used = max(self.q_heads // GROUP, 1)
        self.per_kv = self.q_heads // self.kv_used
        self.width = self.kv_used * HD
        self.reqs = span_ids.shape[0]
        self.source_rows = self.capacity * self.half
        first = -(-self.source_rows // 2 // 128) * 128
        self.chunks = ((0, first), (first, self.source_rows - first))

    def kv_start(self, core):
        return pl.multiple_of(lax.div(core * self.q_heads, GROUP) * HD, HD)

    def partner(self, store, step):
        if self.stores & (self.stores - 1) == 0:
            return store ^ step
        return lax.rem(store + step, self.stores)

    def origin(self, store, step):
        if self.stores & (self.stores - 1) == 0:
            return store ^ step
        return lax.rem(store + self.stores - step, self.stores)

    def pairs(self, step, turn):
        listed = []
        for store in range(self.stores):
            for core in range(self.cores):
                if self.stores & (self.stores - 1) == 0:
                    other = store ^ step
                else:
                    other = (store + step) % self.stores
                listed.append((store * self.cores + core, other * self.cores + (core + turn) % self.cores))
        return listed


def find_spans(plan, ids_ref, slot_ref, source, dest):
    zero = jnp.int32(0)
    places, owners, turns, live = ([zero] * plan.capacity for _ in range(4))
    seen = zero
    for turn in range(NCH):
        for request in range(plan.req_dev):
            slot = slot_ref[ids_ref[(dest * plan.req_dev + request) * NCH + turn]]
            place = slot - source * plan.ch_dev
            hit = (place >= 0) & (place < plan.ch_dev)
            for rank in range(plan.capacity):
                here = hit & (seen == rank)
                places[rank] = jnp.where(here, place, places[rank])
                owners[rank] = jnp.where(here, request, owners[rank])
                turns[rank] = jnp.where(here, turn, turns[rank])
                live[rank] = jnp.where(here, 1, live[rank])
            seen = seen + hit.astype(jnp.int32)
    return places, owners, turns, live


def live_ranks(plan, chosen_ref, dest, core, owners, turns, live):
    lane_request = lax.broadcasted_iota(jnp.int32, chosen_ref.shape, 1)
    lane = lax.broadcasted_iota(jnp.int32, (SEL, plan.half), 1)
    before = (
        lax.broadcasted_iota(jnp.int32, (plan.half, plan.half), 0)
        < lax.broadcasted_iota(jnp.int32, (plan.half, plan.half), 1)
    ).astype(jnp.bfloat16)
    sent = jnp.zeros((1, 1), jnp.float32)
    ranks = []
    for rank in range(plan.capacity):
        request = dest * plan.req_dev + owners[rank]
        column = jnp.sum(jnp.where(lane_request == request, chosen_ref[...], 0), axis=1, keepdims=True)
        base = turns[rank] * SPAN + core * plan.half
        hits = jnp.where(column - base == lane, 1.0, 0.0)
        keep = (1.0 - jnp.sum(hits, axis=0, keepdims=True)) * live[rank].astype(jnp.float32)
        ahead = jnp.dot(
            jnp.broadcast_to(keep, (16, plan.half)).astype(jnp.bfloat16), before,
            preferred_element_type=jnp.float32,
        )[:1]
        ranks.append(jnp.where(keep > 0.5, ahead + sent, -1.0))
        sent = sent + jnp.sum(keep, axis=1, keepdims=True)
    return jnp.concatenate(ranks, axis=1).astype(jnp.int32)


def selection(ranks, row_first, rows):
    wanted = lax.broadcasted_iota(jnp.int32, (rows, ranks.shape[1]), 0) + row_first
    return jnp.where(wanted == ranks, 1.0, 0.0).astype(jnp.bfloat16)


def pack_kernel(plan, step, chunks, ids_ref, slot_ref, chosen_ref, keys_ref, values_ref, *rest):
    outs, (key_rows, value_rows, sems) = rest[: -3], rest[-3:]
    store, core = lax.axis_index("store"), lax.axis_index("sub")
    dest = plan.partner(store, step)
    places, owners, turns, live = find_spans(plan, ids_ref, slot_ref, store, dest)
    copies = []
    for rank in range(plan.capacity):
        rows = pl.ds(rank * plan.half, plan.half)
        copies.append(pltpu.make_async_copy(keys_ref.at[places[rank]], key_rows.at[rows], sems.at[0, rank]))
        copies.append(pltpu.make_async_copy(values_ref.at[places[rank]], value_rows.at[rows], sems.at[1, rank]))
    for copy in copies:
        copy.start()
    ranks = live_ranks(plan, chosen_ref, dest, core, owners, turns, live)
    for copy in copies:
        copy.wait()
    at = 0
    for row_first, rows in chunks:
        select = selection(ranks, row_first, rows)
        for turn in range(plan.cores):
            start = plan.kv_start(lax.rem(core + turn, plan.cores))
            for source, offset in ((key_rows, 0), (value_rows, plan.width)):
                outs[at][:, pl.ds(offset, plan.width)] = jnp.dot(
                    select, source[:, pl.ds(start, plan.width)], preferred_element_type=jnp.float32
                ).astype(jnp.bfloat16)
            at += 1


def pack(plan, step, chunks, ids, slots, chosen, store_keys, store_values):
    shapes = [
        jax.ShapeDtypeStruct((rows, 2 * plan.width), jnp.bfloat16)
        for _, rows in chunks
        for _ in range(plan.cores)
    ]
    return pl.pallas_call(
        functools.partial(pack_kernel, plan, step, chunks),
        out_shape=shapes,
        grid_spec=pltpu.PrefetchScalarGridSpec(
            num_scalar_prefetch=2,
            grid=(1,),
            in_specs=[
                pl.BlockSpec(chosen.shape, lambda i, *_: (0, 0)),
                pl.BlockSpec(memory_space=pl.ANY),
                pl.BlockSpec(memory_space=pl.ANY),
            ],
            out_specs=[pl.BlockSpec(s.shape, lambda i, *_: (0, 0)) for s in shapes],
            scratch_shapes=[
                pltpu.VMEM((plan.source_rows, plan.kv_columns), jnp.bfloat16),
                pltpu.VMEM((plan.source_rows, plan.kv_columns), jnp.bfloat16),
                pltpu.SemaphoreType.DMA((2, plan.capacity)),
            ],
        ),
        cost_estimate=pl.CostEstimate(
            flops=4 * plan.source_rows**2 * plan.kv_columns,
            bytes_accessed=8 * plan.source_rows * plan.kv_columns,
            transcendentals=0,
        ),
        name=f"pack_{step}",
    )(ids, slots, chosen, store_keys, store_values)


def place_kernel(plan, chunks, ids_ref, slot_ref, chosen_ref, *outs):
    place_refs, first_ref = outs[:-1], outs[-1]
    stream = pl.program_id(0)
    store, core = lax.axis_index("store"), lax.axis_index("sub")
    source = plan.origin(store, lax.div(stream, plan.cores))
    turn = lax.rem(stream, plan.cores)
    source_core = lax.rem(core + plan.cores - turn, plan.cores)
    _, owners, turns, live = find_spans(plan, ids_ref, slot_ref, source, store)
    ranks = live_ranks(plan, chosen_ref, store, source_core, owners, turns, live)
    lane = lax.broadcasted_iota(jnp.int32, (1, plan.half), 1)
    tables = [[], [], []]
    for rank in range(plan.capacity):
        position = turns[rank] * SPAN + source_core * plan.half + lane
        tables[0].append(position >> 8)
        tables[1].append(position & 255)
        tables[2].append(jnp.broadcast_to(owners[rank] + 1, (1, plan.half)))
    table = jnp.concatenate(
        [jnp.concatenate(one, axis=1) for one in tables]
        + [jnp.zeros((13, plan.source_rows), jnp.int32)],
        axis=0,
    ).astype(jnp.float32).astype(jnp.bfloat16)
    for at, (row_first, rows) in enumerate(chunks):
        found = lax.dot_general(
            table, selection(ranks, row_first, rows), (((1,), (1,)), ((), ())),
            preferred_element_type=jnp.float32,
        )
        position = (found[0:1] * 256.0 + found[1:2]).astype(jnp.int32)
        owner = found[2:3].astype(jnp.int32)
        for request in range(plan.req_dev):
            own = jnp.where(owner == request + 1, position, FAR)
            place_refs[at][0, request] = own
            first_ref[(stream * len(chunks) + at) * plan.req_dev + request] = jnp.min(own)


def place(plan, chunks, ids, slots, chosen):
    streams = plan.stores * plan.cores
    shapes = [
        jax.ShapeDtypeStruct((streams, plan.req_dev, 1, rows), jnp.int32) for _, rows in chunks
    ]
    specs = [pl.BlockSpec((1,) + s.shape[1:], lambda i, *_: (i, 0, 0, 0)) for s in shapes]
    shapes.append(jax.ShapeDtypeStruct((streams * len(chunks) * plan.req_dev,), jnp.int32))
    specs.append(pl.BlockSpec(memory_space=pltpu.SMEM))
    return pl.pallas_call(
        functools.partial(place_kernel, plan, chunks),
        out_shape=shapes,
        grid_spec=pltpu.PrefetchScalarGridSpec(
            num_scalar_prefetch=2,
            grid=(streams,),
            in_specs=[pl.BlockSpec(chosen.shape, lambda i, *_: (0, 0))],
            out_specs=specs,
        ),
        cost_estimate=pl.CostEstimate(
            flops=32 * streams * plan.source_rows**2, bytes_accessed=1 << 18, transcendentals=0
        ),
        name="place",
    )(ids, slots, chosen)


def attend_kernel(plan, opening, closing, blocks, *refs):
    refs = list(refs)
    pos_ref, first_ref, len_ref = refs[:3]
    at = 3
    query_ref, column_ref = refs[at : at + 2]
    at += 2
    if opening:
        fresh_key_ref, fresh_value_ref = refs[at : at + 2]
        at += 2
    else:
        total_in, stats_in = refs[at : at + 2]
        at += 2
    streams = refs[at : at + len(blocks)]
    at += len(blocks)
    places = refs[at : at + len(blocks)]
    at += len(blocks)
    if closing:
        out_ref = refs[at]
        at += 1
        total_ref = refs[at]
        at += 1
    else:
        total_ref, stats_ref = refs[at : at + 2]
        at += 2
    top, sums = refs[at : at + 2]
    request, tile = pl.program_id(0), pl.program_id(1)
    core = lax.axis_index("sub")
    heads = plan.q_heads
    bunch = min(4, plan.per_kv)
    if not opening:
        for head in range(heads):
            top[head] = jnp.broadcast_to(stats_in[0, :, head : head + 1], (TILE, HD))
            sums[head] = jnp.broadcast_to(stats_in[0, :, 64 + head : 65 + head], (TILE, HD))

    def head_at(head):
        return pl.ds(pl.multiple_of(head * HD, HD), HD)

    def block(index, key, value, allowed, starting):
        extended = jnp.concatenate([value, jnp.ones(value.shape, jnp.bfloat16)], axis=1)
        for member in range(bunch):
            head = index * bunch + member
            lanes = head_at(head)
            scores = lax.dot_general(
                query_ref[0, :, lanes], key, (((1,), (1,)), ((), ())),
                preferred_element_type=jnp.float32,
            )
            scores = jnp.where(allowed, scores, NEGATIVE)
            largest = jnp.max(scores, axis=1, keepdims=True)
            if starting:
                new_top = jnp.broadcast_to(largest, (TILE, HD))
            else:
                old_top = top[head]
                new_top = jnp.maximum(old_top, largest)
            powers = jnp.exp2((scores - new_top[:, :1]) * LOG_SCALE).astype(jnp.bfloat16)
            update = jnp.dot(powers, extended, preferred_element_type=jnp.float32)
            if starting:
                total_ref[0, :, lanes] = update[:, :HD]
                sums[head] = update[:, HD:]
            else:
                factor = jnp.exp2((old_top - new_top) * LOG_SCALE)
                total_ref[0, :, lanes] = total_ref[0, :, lanes] * factor + update[:, :HD]
                sums[head] = sums[head] * factor + update[:, HD:]
            top[head] = new_top

    last_pos = pos_ref[request * ROWS + (tile + 1) * TILE - 1]

    def bunch_step(index, unused):
        kv = lax.div(index * bunch, plan.per_kv)
        if opening:
            lanes = pl.ds(pl.multiple_of(plan.kv_start(core) + kv * HD, HD), HD)
            row = lax.broadcasted_iota(jnp.int32, (TILE, ROWS), 0) + tile * TILE
            allowed = lax.broadcasted_iota(jnp.int32, (TILE, ROWS), 1) <= row
            block(index, fresh_key_ref[0, :, lanes], fresh_value_ref[0, :, lanes], allowed, True)
        else:
            for member in range(bunch):
                lanes = head_at(index * bunch + member)
                total_ref[0, :, lanes] = total_in[0, :, lanes]
        key_lanes = pl.ds(pl.multiple_of(kv * HD, HD), HD)
        value_lanes = pl.ds(pl.multiple_of(plan.width + kv * HD, HD), HD)
        for number, (stream, chunk) in enumerate(blocks):
            @pl.when(first_ref[(stream * len(plan.chunks) + chunk) * plan.req_dev + request] <= last_pos)
            def _(number=number):
                allowed = places[number][0, 0] <= column_ref[0]
                block(
                    index, streams[number][:, key_lanes], streams[number][:, value_lanes], allowed, False
                )
        return unused

    lax.fori_loop(0, heads // bunch, bunch_step, 0)

    if closing:
        row = lax.broadcasted_iota(jnp.int32, (TILE, HD), 0) + tile * TILE
        live = row < SEL + len_ref[request]

        def close(head, unused):
            lanes = head_at(head)
            out_ref[0, :, lanes] = jnp.where(live, total_ref[0, :, lanes] / sums[head], 0.0).astype(jnp.bfloat16)
            return unused

        lax.fori_loop(0, heads, close, 0)
    else:
        lane = lax.broadcasted_iota(jnp.int32, (TILE, HD), 1)
        stats = jnp.zeros((TILE, HD), jnp.float32)
        for head in range(heads):
            stats = jnp.where(lane == head, top[head], stats)
            stats = jnp.where(lane == 64 + head, sums[head], stats)
        stats_ref[0] = stats


def attend(plan, state, closing, blocks, arrays, places, firsts, fresh, pos, pos_column, lengths):
    opening = state is None
    fresh_query, fresh_keys, fresh_values = fresh
    req_dev = plan.req_dev
    row_block = lambda width: pl.BlockSpec((1, TILE, width), lambda r, t, *_: (r, t, 0))
    operands = [pos, firsts, lengths, fresh_query, pos_column]
    specs = [row_block(plan.q_columns), row_block(1)]
    aliases = {}
    if opening:
        operands += [fresh_keys, fresh_values]
        specs += [pl.BlockSpec((1, ROWS, plan.kv_columns), lambda r, t, *_: (r, 0, 0))] * 2
    else:
        operands += list(state)
        specs += [row_block(plan.q_columns), row_block(HD)]
        if not closing:
            aliases = {5: 0, 6: 1}
    for array in arrays:
        operands.append(array)
        specs.append(pl.BlockSpec(array.shape, lambda r, t, *_: (0, 0)))
    for stream, chunk in blocks:
        operands.append(places[chunk])
        specs.append(
            pl.BlockSpec(
                (1, 1, 1, places[chunk].shape[3]), lambda r, t, *_, stream=stream: (stream, r, 0, 0)
            )
        )
    scratch = [pltpu.VMEM((plan.q_heads, TILE, HD), jnp.float32)] * 2
    if closing:
        out_shape = jax.ShapeDtypeStruct(fresh_query.shape, jnp.bfloat16)
        out_specs = row_block(plan.q_columns)
        scratch = [pltpu.VMEM((1, TILE, plan.q_columns), jnp.float32)] + scratch
    else:
        out_shape = [
            jax.ShapeDtypeStruct((req_dev, ROWS, plan.q_columns), jnp.float32),
            jax.ShapeDtypeStruct((req_dev, ROWS, HD), jnp.float32),
        ]
        out_specs = [row_block(plan.q_columns), row_block(HD)]
    keys = sum(array.shape[0] for array in arrays) // 2 + (ROWS * req_dev if opening else 0)
    return pl.pallas_call(
        functools.partial(attend_kernel, plan, opening, closing, blocks),
        out_shape=out_shape,
        grid_spec=pltpu.PrefetchScalarGridSpec(
            num_scalar_prefetch=3,
            grid=(req_dev, ROWS // TILE),
            in_specs=specs,
            out_specs=out_specs,
            scratch_shapes=scratch,
        ),
        input_output_aliases=aliases,
        cost_estimate=pl.CostEstimate(
            flops=8 * keys * ROWS * plan.q_heads * HD,
            bytes_accessed=req_dev * ROWS * plan.q_columns * 10,
            transcendentals=keys * ROWS * plan.q_heads,
        ),
        name=f"attend_{blocks[0][0]}_{blocks[0][1]}",
    )(*operands)


def body(
    fresh_query,
    fresh_keys,
    fresh_values,
    store_keys,
    store_values,
    span_ids,
    span_slot,
    select_pos,
    ask_len,
):
    plan = Plan(fresh_query, fresh_keys, store_keys, span_ids, span_slot)
    store_index = lax.axis_index("store")
    ids = span_ids.reshape(-1)
    chosen = jnp.transpose(select_pos)
    chunks = plan.chunks
    steps = list(range(1, plan.stores))
    if plan.stores == 4:
        steps = [2, 1, 3]
    arrived = {}
    for step in steps[:1] + [0] + steps[1:]:
        packed = pack(plan, step, chunks, ids, span_slot, chosen, store_keys, store_values)
        at = 0
        for chunk in range(len(chunks)):
            for turn in range(plan.cores):
                block = packed[at]
                at += 1
                if step != 0 or turn != 0:
                    block = lax.ppermute(block, ("store", "sub"), plan.pairs(step, turn))
                arrived[(step * plan.cores + turn, chunk)] = block
    *places, firsts = place(plan, chunks, ids, span_slot, chosen)
    my_pos = lax.dynamic_slice_in_dim(select_pos, store_index * plan.req_dev, plan.req_dev, 0)
    lengths = lax.dynamic_slice_in_dim(ask_len, store_index * plan.req_dev, plan.req_dev, 0)
    asked = jnp.broadcast_to(CTX + jnp.arange(QLEN, dtype=jnp.int32), (plan.req_dev, QLEN))
    pos = jnp.concatenate([my_pos, asked], axis=1)
    pos_column = pos[:, :, None]
    pos = pos.reshape(-1)

    def both(step, chunk_list):
        return [(step * plan.cores + turn, chunk) for chunk in chunk_list for turn in range(plan.cores)]

    everything = list(range(len(chunks)))
    stages = [both(0, everything)]
    for step in steps[:-1]:
        stages.append(both(step, everything))
    stages += [both(steps[-1], [chunk]) for chunk in everything]
    state = None
    for number, blocks in enumerate(stages):
        state = attend(
            plan, state, number == len(stages) - 1, blocks, [arrived[b] for b in blocks], places, firsts,
            (fresh_query, fresh_keys, fresh_values), pos, pos_column, lengths,
        )
    return state


def solution(mesh):
    placed = (
        P(("groups", "store"), None, ("head", "sub")),
        P(("groups", "store"), None, "head"),
        P(("groups", "store"), None, "head"),
        P(("groups", "store"), "sub", "head"),
        P(("groups", "store"), "sub", "head"),
        P("groups", None),
        P("groups"),
        P("groups", None),
        P("groups"),
    )
    return jax.shard_map(
        body,
        mesh=mesh,
        in_specs=placed,
        out_specs=P(("groups", "store"), None, ("head", "sub")),
        check_vma=False,
    )
```

```python
import functools
import math

import jax
import jax.numpy as jnp
from jax import lax
from jax.experimental import pallas as pl
from jax.experimental.pallas import tpu as pltpu
from jax.sharding import PartitionSpec as P

HD = 128
GROUP = 8
SPAN = 512
NCH = 6
CTX = 3072
SEL = 464
QLEN = 64
ROWS = 528

NEGATIVE = -1e30
LIMIT = 2.0**100
TILE = 176
BUNCH = 4
LOG_SCALE = HD ** (-0.5) * math.log2(math.e)


class Plan:
    def __init__(self, fresh_query, fresh_keys, store_keys, span_ids, span_slot):
        self.stores = lax.axis_size("store")
        self.cores = lax.axis_size("sub")
        self.req_dev = fresh_query.shape[0]
        self.ch_dev, self.half, self.kv_columns = store_keys.shape
        self.refs = self.req_dev * NCH
        self.capacity = (self.refs + self.stores - 1) // self.stores
        self.q_columns = fresh_query.shape[2]
        self.q_heads = self.q_columns // HD
        self.kv_used = max(self.q_heads // GROUP, 1)
        self.per_kv = self.q_heads // self.kv_used
        self.width = self.kv_used * HD
        self.reqs = span_ids.shape[0]
        self.source_rows = self.capacity * self.half
        self.chunks = ((0, self.source_rows),)
        if self.capacity > 1:
            first = (self.capacity - 1) * self.half
            self.chunks = ((0, first), (first, self.source_rows - first))

    def kv_start(self, core):
        return pl.multiple_of(lax.div(core * self.q_heads, GROUP) * HD, HD)

    def partner(self, store, step):
        if self.stores & (self.stores - 1) == 0:
            return store ^ step
        return lax.rem(store + step, self.stores)

    def origin(self, store, step):
        if self.stores & (self.stores - 1) == 0:
            return store ^ step
        return lax.rem(store + self.stores - step, self.stores)

    def pairs(self, step, turn):
        listed = []
        for store in range(self.stores):
            for core in range(self.cores):
                if self.stores & (self.stores - 1) == 0:
                    other = store ^ step
                else:
                    other = (store + step) % self.stores
                listed.append((store * self.cores + core, other * self.cores + (core + turn) % self.cores))
        return listed


def find_spans(plan, ids_ref, slot_ref, source, dest):
    zero = jnp.int32(0)
    places, owners, turns, live = ([zero] * plan.capacity for _ in range(4))
    seen = zero
    for turn in range(NCH):
        for request in range(plan.req_dev):
            slot = slot_ref[ids_ref[(dest * plan.req_dev + request) * NCH + turn]]
            place = slot - source * plan.ch_dev
            hit = (place >= 0) & (place < plan.ch_dev)
            for rank in range(plan.capacity):
                here = hit & (seen == rank)
                places[rank] = jnp.where(here, place, places[rank])
                owners[rank] = jnp.where(here, request, owners[rank])
                turns[rank] = jnp.where(here, turn, turns[rank])
                live[rank] = jnp.where(here, 1, live[rank])
            seen = seen + hit.astype(jnp.int32)
    return places, owners, turns, live


def live_ranks(plan, chosen_ref, dest, core, owners, turns, live):
    lane_request = lax.broadcasted_iota(jnp.int32, chosen_ref.shape, 1)
    lane = lax.broadcasted_iota(jnp.int32, (SEL, plan.half), 1)
    before = (
        lax.broadcasted_iota(jnp.int32, (plan.half, plan.half), 0)
        < lax.broadcasted_iota(jnp.int32, (plan.half, plan.half), 1)
    ).astype(jnp.bfloat16)
    sent = jnp.zeros((1, 1), jnp.float32)
    ranks = []
    for rank in range(plan.capacity):
        request = dest * plan.req_dev + owners[rank]
        column = jnp.sum(jnp.where(lane_request == request, chosen_ref[...], 0), axis=1, keepdims=True)
        base = turns[rank] * SPAN + core * plan.half
        hits = jnp.where(column - base == lane, 1.0, 0.0)
        keep = (1.0 - jnp.sum(hits, axis=0, keepdims=True)) * live[rank].astype(jnp.float32)
        ahead = jnp.dot(
            jnp.broadcast_to(keep, (16, plan.half)).astype(jnp.bfloat16), before,
            preferred_element_type=jnp.float32,
        )[:1]
        ranks.append(jnp.where(keep > 0.5, ahead + sent, -1.0))
        sent = sent + jnp.sum(keep, axis=1, keepdims=True)
    return jnp.concatenate(ranks, axis=1).astype(jnp.int32)


def selection(ranks, row_first, rows):
    wanted = lax.broadcasted_iota(jnp.int32, (rows, ranks.shape[1]), 0) + row_first
    return jnp.where(wanted == ranks, 1.0, 0.0).astype(jnp.bfloat16)


def pack_kernel(plan, step, chunks, ids_ref, slot_ref, chosen_ref, keys_ref, values_ref, *rest):
    outs, (key_rows, value_rows, sems) = rest[: -3], rest[-3:]
    store, core = lax.axis_index("store"), lax.axis_index("sub")
    dest = plan.partner(store, step)
    places, owners, turns, live = find_spans(plan, ids_ref, slot_ref, store, dest)
    copies = []
    for rank in range(plan.capacity):
        rows = pl.ds(rank * plan.half, plan.half)
        copies.append(pltpu.make_async_copy(keys_ref.at[places[rank]], key_rows.at[rows], sems.at[0, rank]))
        copies.append(pltpu.make_async_copy(values_ref.at[places[rank]], value_rows.at[rows], sems.at[1, rank]))
    for copy in copies:
        copy.start()
    ranks = live_ranks(plan, chosen_ref, dest, core, owners, turns, live)
    for copy in copies:
        copy.wait()
    at = 0
    for row_first, rows in chunks:
        select = selection(ranks, row_first, rows)
        for turn in range(plan.cores):
            start = plan.kv_start(lax.rem(core + turn, plan.cores))
            for source, offset in ((key_rows, 0), (value_rows, plan.width)):
                outs[at][:, pl.ds(offset, plan.width)] = jnp.dot(
                    select, source[:, pl.ds(start, plan.width)], preferred_element_type=jnp.float32
                ).astype(jnp.bfloat16)
            at += 1


def pack(plan, step, chunks, ids, slots, chosen, store_keys, store_values):
    shapes = [
        jax.ShapeDtypeStruct((rows, 2 * plan.width), jnp.bfloat16)
        for _, rows in chunks
        for _ in range(plan.cores)
    ]
    return pl.pallas_call(
        functools.partial(pack_kernel, plan, step, chunks),
        out_shape=shapes,
        grid_spec=pltpu.PrefetchScalarGridSpec(
            num_scalar_prefetch=2,
            grid=(1,),
            in_specs=[
                pl.BlockSpec(chosen.shape, lambda i, *_: (0, 0)),
                pl.BlockSpec(memory_space=pl.ANY),
                pl.BlockSpec(memory_space=pl.ANY),
            ],
            out_specs=[pl.BlockSpec(s.shape, lambda i, *_: (0, 0)) for s in shapes],
            scratch_shapes=[
                pltpu.VMEM((plan.source_rows, plan.kv_columns), jnp.bfloat16),
                pltpu.VMEM((plan.source_rows, plan.kv_columns), jnp.bfloat16),
                pltpu.SemaphoreType.DMA((2, plan.capacity)),
            ],
        ),
        cost_estimate=pl.CostEstimate(
            flops=4 * plan.source_rows**2 * plan.kv_columns,
            bytes_accessed=8 * plan.source_rows * plan.kv_columns,
            transcendentals=0,
        ),
        name=f"pack_{step}",
    )(ids, slots, chosen, store_keys, store_values)


def spans_before(position_row, start):
    return jnp.sum(jnp.where(position_row < start, 1.0, 0.0), axis=1, keepdims=True)


def blend(plan, stage, table, my_pos_ref, fresh_key_ref, fresh_value_ref, streams, keys, values):
    core = lax.axis_index("sub")
    start = plan.kv_start(core)
    columns = pl.ds(start, plan.width)
    for turn in range(plan.cores):
        source_core = lax.rem(core + plan.cores - turn, plan.cores)
        offset = jnp.zeros((1, 1), jnp.float32)
        for rank in range(max(stage.ranks) + 1):
            owner, base = table[2 * rank], table[2 * rank + 1] + source_core * plan.half
            live = owner >= 0
            request = jnp.maximum(owner, 0)
            listed = my_pos_ref[pl.ds(request, 1), :]
            first = spans_before(listed, base)
            taken = spans_before(listed, base + plan.half) - first
            if rank in stage.ranks:
                at = stage.ranks.index(rank)

                @pl.when(live)
                def _(at=at, offset=offset, first=first, listed=listed, base=base, request=request):
                    token = lax.broadcasted_iota(jnp.int32, (plan.half, SEL), 0) + base
                    same = jnp.where(listed == token, 1.0, 0.0)
                    ahead = jnp.sum(jnp.where(listed < token, 1.0, 0.0), axis=1, keepdims=True)
                    chosen = jnp.sum(same, axis=1, keepdims=True)
                    row = lax.broadcasted_iota(jnp.int32, (plan.half, 1), 0).astype(jnp.float32)
                    row = row + offset - ahead + first
                    row = jnp.where(chosen > 0.5, -1.0, row).astype(jnp.int32)
                    fresh_pick = same.astype(jnp.bfloat16)
                    key = jnp.dot(fresh_pick, fresh_key_ref[request, :SEL, columns], preferred_element_type=jnp.float32)
                    value = jnp.dot(fresh_pick, fresh_value_ref[request, :SEL, columns], preferred_element_type=jnp.float32)
                    for number, chunk in enumerate(stage.chunks):
                        row_first, rows = plan.chunks[chunk]
                        lane = lax.broadcasted_iota(jnp.int32, (plan.half, rows), 1) + row_first
                        pick = jnp.where(lane == row, 1.0, 0.0).astype(jnp.bfloat16)
                        stream = streams[number * plan.cores + turn]
                        key = key + jnp.dot(pick, stream[:, : plan.width], preferred_element_type=jnp.float32)
                        value = value + jnp.dot(pick, stream[:, plan.width :], preferred_element_type=jnp.float32)
                    place = pl.ds(pl.multiple_of(source_core * plan.half, plan.half), plan.half)
                    keys[at, place, :] = key.astype(jnp.bfloat16)
                    values[at, place, :] = value.astype(jnp.bfloat16)

            offset = offset + (plan.half - taken) * live.astype(jnp.float32)


def attend_kernel(plan, stage, *refs):
    refs = list(refs)

    def take(count):
        taken = refs[:count]
        del refs[:count]
        return taken

    ids_ref, slot_ref, pos_ref, len_ref = take(4)
    query_ref, column_ref, my_pos_ref, fresh_key_ref, fresh_value_ref = take(5)
    if not stage.opening:
        total_in, stats_in = take(2)
    streams = take(len(stage.chunks) * plan.cores)
    if stage.closing:
        (out_ref,) = take(1)
        (total_ref,) = take(1)
    else:
        total_ref, stats_ref = take(2)
    keys, values, top, sums, table = take(5)
    request, tile = pl.program_id(0), pl.program_id(1)
    store, core = lax.axis_index("store"), lax.axis_index("sub")
    heads = plan.q_heads
    span = plan.half * plan.cores

    @pl.when((request == 0) & (tile == 0))
    def _():
        source = plan.origin(store, stage.step)
        _, owners, turns, live = find_spans(plan, ids_ref, slot_ref, source, store)
        for rank in range(plan.capacity):
            table[2 * rank] = jnp.where(live[rank] > 0, owners[rank], -1)
            table[2 * rank + 1] = turns[rank] * SPAN
        blend(plan, stage, table, my_pos_ref, fresh_key_ref, fresh_value_ref, streams, keys, values)

    first_pos = pos_ref[request * ROWS + tile * TILE]
    last_pos = pos_ref[request * ROWS + (tile + 1) * TILE - 1]
    column = column_ref[0]
    start = plan.kv_start(core)

    def head_at(head):
        return pl.ds(pl.multiple_of(head * HD, HD), HD)

    def kv_at(head):
        return pl.ds(pl.multiple_of(lax.div(head, plan.per_kv) * HD, HD), HD)

    def begin():
        if stage.opening:
            rows = pl.ds(pl.multiple_of(tile * TILE, 16), TILE)
            total_ref[...] = jnp.zeros_like(total_ref)
            sums[...] = jnp.zeros_like(sums)
            for head in range(heads):
                lanes = pl.ds(start + head // plan.per_kv * HD, HD)
                own = fresh_key_ref[request, rows, lanes].astype(jnp.float32)
                product = query_ref[0, :, head * HD : (head + 1) * HD].astype(jnp.float32) * own
                top[head] = jnp.broadcast_to(jnp.sum(product, axis=1, keepdims=True), (TILE, HD))
        else:
            total_ref[...] = total_in[...]
            for head in range(heads):
                top[head] = jnp.broadcast_to(stats_in[0, :, head : head + 1], (TILE, HD))
                sums[head] = jnp.broadcast_to(stats_in[0, :, 64 + head : 65 + head], (TILE, HD))

    def wide(array, width):
        return jnp.concatenate([array] * (width // HD), axis=1)

    def quick(head, key, extended, allowed):
        lanes = head_at(head)
        scores = lax.dot_general(
            query_ref[0, :, lanes], key, (((1,), (1,)), ((), ())), preferred_element_type=jnp.float32
        )
        powers = jnp.exp2((scores - wide(top[head], key.shape[0])) * LOG_SCALE)
        if allowed is not None:
            powers = jnp.where(allowed, powers, 0.0)
        update = jnp.dot(powers.astype(jnp.bfloat16), extended, preferred_element_type=jnp.float32)
        total_ref[0, :, lanes] += update[:, :HD]
        sums[head] += update[:, HD:]

    def careful(head, key, extended, allowed):
        lanes = head_at(head)
        scores = lax.dot_general(
            query_ref[0, :, lanes], key, (((1,), (1,)), ((), ())), preferred_element_type=jnp.float32
        )
        scores = jnp.where(allowed, scores, NEGATIVE)
        old_top = top[head]
        new_top = jnp.maximum(old_top, jnp.max(scores, axis=1, keepdims=True))
        powers = jnp.exp2((scores - wide(new_top, key.shape[0])) * LOG_SCALE)
        update = jnp.dot(powers.astype(jnp.bfloat16), extended, preferred_element_type=jnp.float32)
        factor = jnp.exp2((old_top - new_top) * LOG_SCALE)
        total_ref[0, :, lanes] = total_ref[0, :, lanes] * factor + update[:, :HD]
        sums[head] = sums[head] * factor + update[:, HD:]
        top[head] = new_top

    def extend(value):
        return jnp.concatenate([value, jnp.ones(value.shape, jnp.bfloat16)], axis=1)

    def over_heads(act, bunch, at, allowed):
        def step(index, unused):
            key = keys[at, :, kv_at(index * bunch)]
            extended = extend(values[at, :, kv_at(index * bunch)])
            for member in range(bunch):
                act(index * bunch + member, key, extended, allowed)
            return unused

        lax.fori_loop(0, heads // bunch, step, 0)

    def asked(act):
        lane = lax.broadcasted_iota(jnp.int32, (TILE, 2 * QLEN), 1)
        allowed = lane + CTX <= column

        def step(head, unused):
            lanes = pl.ds(pl.multiple_of(start + lax.div(head, plan.per_kv) * HD, HD), HD)
            key = fresh_key_ref[request, SEL:, lanes]
            value = fresh_value_ref[request, SEL:, lanes]
            key = jnp.concatenate([key, jnp.zeros_like(key)], axis=0)
            value = jnp.concatenate([value, jnp.zeros_like(value)], axis=0)
            act(head, key, extend(value), allowed)
            return unused

        lax.fori_loop(0, heads, step, 0)

    def mask(base):
        return lax.broadcasted_iota(jnp.int32, (TILE, span), 1) + base <= column

    def run(bunch, act, masked_only):
        for at, rank in enumerate(stage.ranks):
            owner, base = table[2 * rank], table[2 * rank + 1]
            due = (owner == request) & (base <= last_pos)
            clear = base + span - 1 <= first_pos
            if masked_only:
                @pl.when(due)
                def _(at=at, base=base):
                    over_heads(act, bunch, at, mask(base))
            else:
                @pl.when(due & clear)
                def _(at=at):
                    over_heads(act, bunch, at, None)

                @pl.when(due & jnp.logical_not(clear))
                def _(at=at, base=base):
                    over_heads(act, bunch, at, mask(base))
        if stage.opening:
            @pl.when(last_pos >= CTX)
            def _():
                asked(act)

    begin()
    run(min(BUNCH, plan.per_kv), quick, False)

    largest = jnp.max(sums[0])
    for head in range(1, heads):
        largest = jnp.maximum(largest, jnp.max(sums[head]))

    @pl.when(jnp.logical_not(largest < LIMIT))
    def _():
        begin()
        run(1, careful, True)

    if stage.closing:
        row = lax.broadcasted_iota(jnp.int32, (TILE, HD), 0) + tile * TILE
        live = row < SEL + len_ref[request]
        for head in range(heads):
            lanes = slice(head * HD, (head + 1) * HD)
            result = total_ref[0, :, lanes] / sums[head]
            out_ref[0, :, lanes] = jnp.where(live, result, 0.0).astype(jnp.bfloat16)
    else:
        lane = lax.broadcasted_iota(jnp.int32, (TILE, HD), 1)
        stats = jnp.zeros((TILE, HD), jnp.float32)
        for head in range(heads):
            stats = jnp.where(lane == head, top[head], stats)
            stats = jnp.where(lane == 64 + head, sums[head], stats)
        stats_ref[0] = stats


def attend(plan, stage, state, arrays, fresh, ids, slots, my_pos, pos, pos_column, lengths):
    fresh_query, fresh_keys, fresh_values = fresh
    req_dev = plan.req_dev
    row_block = lambda width: pl.BlockSpec((1, TILE, width), lambda r, t, *_: (r, t, 0))
    whole = lambda array: pl.BlockSpec(array.shape, lambda r, t, *_: (0,) * array.ndim)
    operands = [ids, slots, pos, lengths, fresh_query, pos_column, my_pos, fresh_keys, fresh_values]
    specs = [row_block(plan.q_columns), row_block(1)] + [whole(a) for a in operands[6:]]
    aliases = {}
    if not stage.opening:
        if not stage.closing:
            aliases = {len(operands): 0, len(operands) + 1: 1}
        operands += list(state)
        specs += [row_block(plan.q_columns), row_block(HD)]
    operands += arrays
    specs += [whole(a) for a in arrays]
    span = plan.half * plan.cores
    scratch = [pltpu.VMEM((len(stage.ranks), span, plan.width), jnp.bfloat16)] * 2
    scratch += [pltpu.VMEM((plan.q_heads, TILE, HD), jnp.float32)] * 2
    scratch += [pltpu.SMEM((2 * plan.capacity,), jnp.int32)]
    if stage.closing:
        out_shape = jax.ShapeDtypeStruct(fresh_query.shape, jnp.bfloat16)
        out_specs = row_block(plan.q_columns)
        scratch = [pltpu.VMEM((1, TILE, plan.q_columns), jnp.float32)] + scratch
    else:
        out_shape = [
            jax.ShapeDtypeStruct((req_dev, ROWS, plan.q_columns), jnp.float32),
            jax.ShapeDtypeStruct((req_dev, ROWS, HD), jnp.float32),
        ]
        out_specs = [row_block(plan.q_columns), row_block(HD)]
    scores = len(stage.ranks) * span * ROWS * plan.q_heads
    return pl.pallas_call(
        functools.partial(attend_kernel, plan, stage),
        out_shape=out_shape,
        grid_spec=pltpu.PrefetchScalarGridSpec(
            num_scalar_prefetch=4,
            grid=(req_dev, ROWS // TILE),
            in_specs=specs,
            out_specs=out_specs,
            scratch_shapes=scratch,
        ),
        input_output_aliases=aliases,
        cost_estimate=pl.CostEstimate(
            flops=4 * scores * HD,
            bytes_accessed=req_dev * ROWS * plan.q_columns * 10,
            transcendentals=scores,
        ),
        name=f"attend_{stage.step}_{stage.ranks[0]}",
    )(*operands)


class Stage:
    def __init__(self, step, ranks, chunks, opening=False, closing=False):
        self.step, self.ranks, self.chunks = step, ranks, chunks
        self.opening, self.closing = opening, closing


def body(
    fresh_query,
    fresh_keys,
    fresh_values,
    store_keys,
    store_values,
    span_ids,
    span_slot,
    select_pos,
    ask_len,
):
    plan = Plan(fresh_query, fresh_keys, store_keys, span_ids, span_slot)
    store_index = lax.axis_index("store")
    ids = span_ids.reshape(-1)
    chosen = jnp.transpose(select_pos)
    chunks = plan.chunks
    steps = list(range(1, plan.stores))
    if plan.stores == 4:
        steps = [2, 1, 3]
    arrived = {}
    for step in steps[:1] + [0] + steps[1:]:
        packed = pack(plan, step, chunks, ids, span_slot, chosen, store_keys, store_values)
        at = 0
        for chunk in range(len(chunks)):
            for turn in range(plan.cores):
                block = packed[at]
                at += 1
                if step != 0 or turn != 0:
                    block = lax.ppermute(block, ("store", "sub"), plan.pairs(step, turn))
                arrived[(step * plan.cores + turn, chunk)] = block
    my_pos = lax.dynamic_slice_in_dim(select_pos, store_index * plan.req_dev, plan.req_dev, 0)
    lengths = lax.dynamic_slice_in_dim(ask_len, store_index * plan.req_dev, plan.req_dev, 0)
    asked = jnp.broadcast_to(CTX + jnp.arange(QLEN, dtype=jnp.int32), (plan.req_dev, QLEN))
    pos = jnp.concatenate([my_pos, asked], axis=1)
    pos_column = pos[:, :, None]
    pos = pos.reshape(-1)
    all_ranks, all_chunks = list(range(plan.capacity)), list(range(len(chunks)))
    stages = [Stage(step, all_ranks, all_chunks) for step in [0] + steps]
    stages[0].opening = True
    if len(chunks) > 1:
        stages[-1:] = [
            Stage(steps[-1], all_ranks[:-1], all_chunks[:-1]),
            Stage(steps[-1], all_ranks[-1:], all_chunks),
        ]
    stages[-1].closing = True
    state = None
    for stage in stages:
        arrays = [
            arrived[(stage.step * plan.cores + turn, chunk)]
            for chunk in stage.chunks
            for turn in range(plan.cores)
        ]
        state = attend(
            plan, stage, state, arrays, (fresh_query, fresh_keys, fresh_values), ids, span_slot,
            my_pos, pos, pos_column, lengths,
        )
    return state


def solution(mesh):
    placed = (
        P(("groups", "store"), None, ("head", "sub")),
        P(("groups", "store"), None, "head"),
        P(("groups", "store"), None, "head"),
        P(("groups", "store"), "sub", "head"),
        P(("groups", "store"), "sub", "head"),
        P("groups", None),
        P("groups"),
        P("groups", None),
        P("groups"),
    )
    return jax.shard_map(
        body,
        mesh=mesh,
        in_specs=placed,
        out_specs=P(("groups", "store"), None, ("head", "sub")),
        check_vma=False,
    )
```

```python
import functools
import math

import jax
import jax.numpy as jnp
from jax import lax
from jax.experimental import pallas as pl
from jax.experimental.pallas import tpu as pltpu
from jax.sharding import PartitionSpec as P

HD = 128
GROUP = 8
SPAN = 512
NCH = 6
CTX = 3072
SEL = 464
QLEN = 64
ROWS = 528

NEGATIVE = -1e30
LIMIT = 108.0
TILE = 48
LOG_SCALE = HD ** (-0.5) * math.log2(math.e)


class Plan:
    def __init__(self, fresh_query, fresh_keys, store_keys, span_ids, span_slot):
        self.stores = lax.axis_size("store")
        self.cores = lax.axis_size("sub")
        self.req_dev = fresh_query.shape[0]
        self.ch_dev, self.half, self.kv_columns = store_keys.shape
        self.refs = self.req_dev * NCH
        self.capacity = (self.refs + self.stores - 1) // self.stores
        self.q_columns = fresh_query.shape[2]
        self.q_heads = self.q_columns // HD
        self.kv_used = max(self.q_heads // GROUP, 1)
        self.per_kv = self.q_heads // self.kv_used
        self.width = self.kv_used * HD
        self.reqs = span_ids.shape[0]
        self.source_rows = self.capacity * self.half
        self.sent_rows = self.source_rows
        self.chunks = ((0, self.sent_rows),)
        self.split = self.chunks
        if self.capacity > 1:
            first = (self.capacity - 1) * self.half
            self.split = ((0, first), (first, self.sent_rows - first))
        self.kv_block = lax.div(lax.axis_index("sub") * self.q_heads, GROUP * self.kv_used)

    def kv_start(self, core):
        return pl.multiple_of(lax.div(core * self.q_heads, GROUP) * HD, HD)

    def partner(self, store, step):
        if self.stores & (self.stores - 1) == 0:
            return store ^ step
        return lax.rem(store + step, self.stores)

    def origin(self, store, step):
        if self.stores & (self.stores - 1) == 0:
            return store ^ step
        return lax.rem(store + self.stores - step, self.stores)

    def pairs(self, step, turn):
        listed = []
        for store in range(self.stores):
            for core in range(self.cores):
                if self.stores & (self.stores - 1) == 0:
                    other = store ^ step
                else:
                    other = (store + step) % self.stores
                listed.append((store * self.cores + core, other * self.cores + (core + turn) % self.cores))
        return listed


def find_spans(plan, ids_ref, slot_ref, source, dest):
    zero = jnp.int32(0)
    places, owners, turns, live = ([zero] * plan.capacity for _ in range(4))
    seen = zero
    for turn in range(NCH):
        for request in range(plan.req_dev):
            slot = slot_ref[ids_ref[(dest * plan.req_dev + request) * NCH + turn]]
            place = slot - source * plan.ch_dev
            hit = (place >= 0) & (place < plan.ch_dev)
            for rank in range(plan.capacity):
                here = hit & (seen == rank)
                places[rank] = jnp.where(here, place, places[rank])
                owners[rank] = jnp.where(here, request, owners[rank])
                turns[rank] = jnp.where(here, turn, turns[rank])
                live[rank] = jnp.where(here, 1, live[rank])
            seen = seen + hit.astype(jnp.int32)
    return places, owners, turns, live


def live_ranks(plan, chosen_ref, dest, core, owners, turns, live):
    lane_request = lax.broadcasted_iota(jnp.int32, chosen_ref.shape, 1)
    lane = lax.broadcasted_iota(jnp.int32, (SEL, plan.half), 1)
    before = (
        lax.broadcasted_iota(jnp.int32, (plan.half, plan.half), 0)
        < lax.broadcasted_iota(jnp.int32, (plan.half, plan.half), 1)
    ).astype(jnp.bfloat16)
    sent = jnp.zeros((1, 1), jnp.float32)
    ranks = []
    for rank in range(plan.capacity):
        request = dest * plan.req_dev + owners[rank]
        column = jnp.sum(jnp.where(lane_request == request, chosen_ref[...], 0), axis=1, keepdims=True)
        base = turns[rank] * SPAN + core * plan.half
        hits = jnp.where(column - base == lane, 1.0, 0.0)
        keep = (1.0 - jnp.sum(hits, axis=0, keepdims=True)) * live[rank].astype(jnp.float32)
        ahead = jnp.dot(
            jnp.broadcast_to(keep, (16, plan.half)).astype(jnp.bfloat16), before,
            preferred_element_type=jnp.float32,
        )[:1]
        ranks.append(jnp.where(keep > 0.5, ahead + sent, -1.0))
        sent = sent + jnp.sum(keep, axis=1, keepdims=True)
    return jnp.concatenate(ranks, axis=1).astype(jnp.int32)


def selection(ranks, row_first, rows):
    wanted = lax.broadcasted_iota(jnp.int32, (rows, ranks.shape[1]), 0) + row_first
    return jnp.where(wanted == ranks, 1.0, 0.0).astype(jnp.bfloat16)


def pack_kernel(plan, step, chunks, ids_ref, slot_ref, chosen_ref, keys_ref, values_ref, *rest):
    outs, (key_rows, value_rows, sems) = rest[: -3], rest[-3:]
    store, core = lax.axis_index("store"), lax.axis_index("sub")
    dest = plan.partner(store, step)
    places, owners, turns, live = find_spans(plan, ids_ref, slot_ref, store, dest)
    copies = []
    for rank in range(plan.capacity):
        rows = pl.ds(rank * plan.half, plan.half)
        copies.append(pltpu.make_async_copy(keys_ref.at[places[rank]], key_rows.at[rows], sems.at[0, rank]))
        copies.append(pltpu.make_async_copy(values_ref.at[places[rank]], value_rows.at[rows], sems.at[1, rank]))
    for copy in copies:
        copy.start()
    ranks = live_ranks(plan, chosen_ref, dest, core, owners, turns, live)
    for copy in copies:
        copy.wait()
    for row_first, rows in tiles(plan.sent_rows):
        first = row_first // plan.half * plan.half
        select = selection(ranks[:, first:], row_first, rows)
        for turn in range(plan.cores):
            start = plan.kv_start(lax.rem(core + turn, plan.cores))
            for number, (chunk_first, chunk_rows) in enumerate(chunks):
                if chunk_first <= row_first < chunk_first + chunk_rows:
                    out = outs[number * plan.cores + turn]
                    place = slice(row_first - chunk_first, row_first - chunk_first + rows)
            for source, offset in ((key_rows, 0), (value_rows, plan.width)):
                out[place, offset : offset + plan.width] = jnp.dot(
                    select, source[first:, pl.ds(start, plan.width)], preferred_element_type=jnp.float32
                ).astype(jnp.bfloat16)


def tiles(rows, size=256):
    return [(first, min(size, rows - first)) for first in range(0, rows, size)]


def pack(plan, step, chunks, ids, slots, chosen, store_keys, store_values):
    shapes = [
        jax.ShapeDtypeStruct((rows, 2 * plan.width), jnp.bfloat16)
        for _, rows in chunks
        for _ in range(plan.cores)
    ]
    return pl.pallas_call(
        functools.partial(pack_kernel, plan, step, chunks),
        out_shape=shapes,
        grid_spec=pltpu.PrefetchScalarGridSpec(
            num_scalar_prefetch=2,
            grid=(1,),
            in_specs=[
                pl.BlockSpec(chosen.shape, lambda i, *_: (0, 0)),
                pl.BlockSpec(memory_space=pl.ANY),
                pl.BlockSpec(memory_space=pl.ANY),
            ],
            out_specs=[pl.BlockSpec(s.shape, lambda i, *_: (0, 0)) for s in shapes],
            scratch_shapes=[
                pltpu.VMEM((plan.source_rows, plan.kv_columns), jnp.bfloat16),
                pltpu.VMEM((plan.source_rows, plan.kv_columns), jnp.bfloat16),
                pltpu.SemaphoreType.DMA((2, plan.capacity)),
            ],
        ),
        cost_estimate=pl.CostEstimate(
            flops=4 * plan.source_rows**2 * plan.kv_columns,
            bytes_accessed=8 * plan.source_rows * plan.kv_columns,
            transcendentals=0,
        ),
        name=f"pack_{step}",
    )(ids, slots, chosen, store_keys, store_values)


def spans_before(position_row, start):
    return jnp.sum(jnp.where(position_row < start, 1.0, 0.0), axis=1, keepdims=True)


def blend(plan, stage, table, my_pos_ref, fresh_key_ref, fresh_value_ref, streams, keys, values):
    core = lax.axis_index("sub")
    for turn in range(plan.cores):
        source_core = lax.rem(core + plan.cores - turn, plan.cores)
        offset = jnp.zeros((1, 1), jnp.float32)
        for rank in range(max(stage.ranks) + 1):
            owner, base = table[2 * rank], table[2 * rank + 1] + source_core * plan.half
            live = owner >= 0
            request = jnp.maximum(owner, 0)
            listed = my_pos_ref[pl.ds(request, 1), :]
            first = spans_before(listed, base)
            taken = spans_before(listed, base + plan.half) - first
            if rank in stage.ranks:
                at = stage.ranks.index(rank)

                @pl.when(live)
                def _(at=at, offset=offset, first=first, listed=listed, base=base, request=request):
                    token = lax.broadcasted_iota(jnp.int32, (plan.half, SEL), 0) + base
                    same = jnp.where(listed == token, 1.0, 0.0)
                    ahead = jnp.sum(jnp.where(listed < token, 1.0, 0.0), axis=1, keepdims=True)
                    chosen = jnp.sum(same, axis=1, keepdims=True)
                    row = lax.broadcasted_iota(jnp.int32, (plan.half, 1), 0).astype(jnp.float32)
                    row = row + offset - ahead + first
                    row = jnp.where(chosen > 0.5, -1.0, row).astype(jnp.int32)
                    fresh_pick = same.astype(jnp.bfloat16)
                    key = jnp.dot(fresh_pick, fresh_key_ref[request, :SEL, :], preferred_element_type=jnp.float32)
                    value = jnp.dot(fresh_pick, fresh_value_ref[request, :SEL, :], preferred_element_type=jnp.float32)
                    if len(stage.chunks) == 1 and plan.sent_rows >= plan.half + 16:
                        rows = plan.half + 16
                        below = jnp.max(offset.astype(jnp.int32)) // 16 * 16
                        below = pl.multiple_of(jnp.minimum(below, plan.sent_rows - rows), 16)
                        parts = [(below, rows, streams[turn], pl.ds(below, rows))]
                    else:
                        parts = [
                            (first_row, rows, streams[number * plan.cores + turn], slice(None))
                            for number, (first_row, rows) in enumerate(stage.chunks)
                        ]
                    for first_row, rows, stream, window in parts:
                        lane = lax.broadcasted_iota(jnp.int32, (plan.half, rows), 1) + first_row
                        pick = jnp.where(lane == row, 1.0, 0.0).astype(jnp.bfloat16)
                        both = jnp.dot(pick, stream[window, :], preferred_element_type=jnp.float32)
                        key = key + both[:, : plan.width]
                        value = value + both[:, plan.width :]
                    place = pl.ds(pl.multiple_of(source_core * plan.half, plan.half), plan.half)
                    keys[at, place, :] = key.astype(jnp.bfloat16)
                    values[at, place, :] = value.astype(jnp.bfloat16)

            offset = offset + (plan.half - taken) * live.astype(jnp.float32)


def attend_kernel(plan, stage, *refs):
    refs = list(refs)

    def take(count):
        taken = refs[:count]
        del refs[:count]
        return taken

    ids_ref, slot_ref, pos_ref, len_ref, _ = take(5)
    column_ref, my_pos_ref, fresh_key_ref, fresh_value_ref = take(4)
    if stage.opening:
        (query_in,) = take(1)
    else:
        query, sizes = take(2)
        take(3)
    streams = take(len(stage.chunks) * plan.cores)
    if stage.closing:
        (out_ref,) = take(1)
    total_ref, sums_ref, top_ref = take(3)
    if stage.opening:
        query, sizes = take(2)
    keys, values, table = take(3)
    request = pl.program_id(0)
    store = lax.axis_index("store")
    span = plan.half * plan.cores
    last = ROWS // TILE
    bunch = plan.per_kv * TILE

    @pl.when(request == 0)
    def _():
        source = plan.origin(store, stage.step)
        _, owners, turns, live = find_spans(plan, ids_ref, slot_ref, source, store)
        for rank in range(plan.capacity):
            table[2 * rank] = jnp.where(live[rank] > 0, owners[rank], -1)
            table[2 * rank + 1] = turns[rank] * SPAN
        blend(plan, stage, table, my_pos_ref, fresh_key_ref, fresh_value_ref, streams, keys, values)

    def rows_of(tile):
        return pl.ds(pl.multiple_of(tile * TILE, 16), TILE)

    def bunch_of(tile, count=1):
        return pl.ds(pl.multiple_of(tile * bunch, 16), count * bunch)

    def members():
        for kv in range(plan.kv_used):
            for member in range(plan.per_kv):
                head = kv * plan.per_kv + member
                yield kv, member, slice(head * HD, (head + 1) * HD)

    if stage.opening:
        def prepare(tile, most):
            long, low = most
            for kv, member, lanes in members():
                place = pl.ds(pl.multiple_of(tile * bunch + member * TILE, 16), TILE)
                taken = query_in[0, rows_of(tile), lanes]
                query[request, kv, place, :] = taken
                taken = taken.astype(jnp.float32)
                own = fresh_key_ref[request, rows_of(tile), kv * HD : (kv + 1) * HD].astype(jnp.float32)
                product = jnp.broadcast_to(jnp.sum(taken * own, axis=1, keepdims=True), (TILE, HD))
                top_ref[request, kv, place, :] = product
                total_ref[request, kv, place, :] = jnp.zeros((TILE, HD), jnp.float32)
                sums_ref[request, kv, place, :] = jnp.zeros((TILE, HD), jnp.float32)
                long = jnp.maximum(long, jnp.sum(jnp.abs(taken), axis=1, keepdims=True))
                low = jnp.maximum(low, -product)
            return long, low

        none = jnp.zeros((TILE, HD), jnp.float32)
        long, low = lax.fori_loop(0, last, prepare, (none, none))
        sizes[request, 0] = long
        sizes[request, 1] = low

    def masks(tile, count, width, base):
        lane = lax.broadcasted_iota(jnp.int32, (TILE, width), 1) + base
        return [lane <= column_ref[0, rows_of(tile + more), :] for more in range(count)]

    def quick(tile, count, kv, key, extended, allowed):
        rows = bunch_of(tile, count)
        scores = lax.dot_general(
            query[request, kv, rows, :], key, (((1,), (1,)), ((), ())), preferred_element_type=jnp.float32
        )
        width = key.shape[0] // HD
        powers = []
        for more in range(count):
            for member in range(plan.per_kv):
                first = more * bunch + member * TILE
                place = pl.ds(pl.multiple_of(tile * bunch + first, 16), TILE)
                shift = jnp.concatenate([top_ref[request, kv, place, :]] * width, axis=1)
                power = jnp.exp2((scores[first : first + TILE] - shift) * LOG_SCALE)
                powers.append(jnp.where(allowed[more], power, 0.0).astype(jnp.bfloat16))
        update = jnp.dot(jnp.concatenate(powers, axis=0), extended, preferred_element_type=jnp.float32)
        total_ref[request, kv, rows, :] += update[:, :HD]
        sums_ref[request, kv, rows, :] += update[:, HD:]

    def careful(tile, count, kv, key, extended, allowed):
        def one(number, unused):
            place = pl.ds(pl.multiple_of(tile * bunch + number * TILE, 16), TILE)
            scores = lax.dot_general(
                query[request, kv, place, :], key, (((1,), (1,)), ((), ())), preferred_element_type=jnp.float32
            )
            scores = jnp.where(allowed[0], scores, NEGATIVE)
            old_top = top_ref[request, kv, place, :]
            new_top = jnp.maximum(old_top, jnp.max(scores, axis=1, keepdims=True))
            shift = jnp.concatenate([new_top] * (key.shape[0] // HD), axis=1)
            powers = jnp.exp2((scores - shift) * LOG_SCALE)
            update = jnp.dot(powers.astype(jnp.bfloat16), extended, preferred_element_type=jnp.float32)
            factor = jnp.exp2((old_top - new_top) * LOG_SCALE)
            total_ref[request, kv, place, :] = total_ref[request, kv, place, :] * factor + update[:, :HD]
            sums_ref[request, kv, place, :] = sums_ref[request, kv, place, :] * factor + update[:, HD:]
            top_ref[request, kv, place, :] = new_top
            return unused

        lax.fori_loop(0, plan.per_kv, one, 0)

    def extend(value):
        return jnp.concatenate([value, jnp.ones(value.shape, jnp.bfloat16)], axis=1)

    def last_pos(tile):
        return pos_ref[request * ROWS + (tile + 1) * TILE - 1]

    def run(act, pairs):
        def span_tiles(at, base, tile, count):
            allowed = masks(tile, count, span, base)
            for kv in range(plan.kv_used):
                lanes = slice(kv * HD, (kv + 1) * HD)
                act(tile, count, kv, keys[at, :, lanes], extend(values[at, :, lanes]), allowed)

        def one_span(at, unused):
            rank = at + stage.ranks[0]
            owner, base = table[2 * rank], table[2 * rank + 1]

            @pl.when(owner == request)
            def _():
                if not pairs:
                    def step(tile, unused):
                        span_tiles(at, base, tile, 1)
                        return unused

                    lax.fori_loop(0, last, step, 0)
                    return

                @pl.when(last_pos(0) >= base)
                def _():
                    span_tiles(at, base, 0, 1)

                first = jnp.int32(0)
                for pair in range(last // 2):
                    first = first + (last_pos(2 * pair + 2) < base).astype(jnp.int32)

                def step(pair, unused):
                    span_tiles(at, base, 2 * pair + 1, 2)
                    return unused

                lax.fori_loop(first, last // 2, step, 0)

            return unused

        lax.fori_loop(0, len(stage.ranks), one_span, 0)
        if stage.opening:
            def ask(tile, unused):
                allowed = masks(tile, 1, 2 * QLEN, CTX)
                for kv in range(plan.kv_used):
                    lanes = slice(kv * HD, (kv + 1) * HD)
                    key, value = fresh_key_ref[request, SEL:, lanes], fresh_value_ref[request, SEL:, lanes]
                    key = jnp.concatenate([key, jnp.zeros_like(key)], axis=0)
                    value = jnp.concatenate([value, jnp.zeros_like(value)], axis=0)
                    act(tile, 1, kv, key, extend(value), allowed)
                return unused

            lax.fori_loop(SEL // TILE, last, ask, 0)

    greatest = jnp.max(jnp.abs(keys[...].astype(jnp.float32)))
    if stage.opening:
        greatest = jnp.maximum(greatest, jnp.max(jnp.abs(fresh_key_ref[request].astype(jnp.float32))))
    reach = (greatest * jnp.max(sizes[request, 0]) + jnp.max(sizes[request, 1])) * LOG_SCALE
    held = reach < LIMIT

    @pl.when(held)
    def _():
        run(quick, True)

    @pl.when(jnp.logical_not(held))
    def _():
        run(careful, False)

    if stage.closing:
        def finish(tile, unused):
            row = lax.broadcasted_iota(jnp.int32, (TILE, HD), 0) + tile * TILE
            live = row < SEL + len_ref[request]
            for kv, member, lanes in members():
                place = pl.ds(pl.multiple_of(tile * bunch + member * TILE, 16), TILE)
                result = total_ref[request, kv, place, :] / sums_ref[request, kv, place, :]
                out_ref[0, rows_of(tile), lanes] = jnp.where(live, result, 0.0).astype(jnp.bfloat16)
            return unused

        lax.fori_loop(0, last, finish, 0)


def attend(plan, stage, state, arrays, fresh, ids, slots, my_pos, pos, pos_column, lengths):
    fresh_query, fresh_keys, fresh_values = fresh
    req_dev = plan.req_dev
    row_block = lambda width: pl.BlockSpec((1, ROWS, width), lambda r, *_: (r, 0, 0))
    whole = lambda array: pl.BlockSpec(array.shape, lambda r, *_: (0,) * array.ndim)
    kept = pl.BlockSpec(memory_space=pltpu.VMEM)
    fresh_block = pl.BlockSpec((req_dev, ROWS, plan.width), lambda r, *s: (0, 0, s[4][0]))
    kv_block = jnp.reshape(plan.kv_block, (1,))
    operands = [ids, slots, pos, lengths, kv_block, pos_column, my_pos, fresh_keys, fresh_values]
    specs = [row_block(1), whole(my_pos), fresh_block, fresh_block]
    aliases = {}
    stacked = (req_dev, plan.kv_used, plan.q_heads // plan.kv_used * ROWS, HD)
    out_shape, out_specs = [], []
    if stage.closing:
        out_shape = [jax.ShapeDtypeStruct(fresh_query.shape, jnp.bfloat16)]
        out_specs = [row_block(plan.q_columns)]
    if stage.opening:
        operands.append(fresh_query)
        specs.append(row_block(plan.q_columns))
    else:
        aliases = {len(operands) + 2 + i: len(out_shape) + i for i in range(3)}
        operands += [state[3], state[4], *state[:3]]
        specs += [kept] * 5
    operands += arrays
    specs += [whole(a) for a in arrays]
    span = plan.half * plan.cores
    scratch = [pltpu.VMEM((len(stage.ranks), span, plan.width), jnp.bfloat16)] * 2
    scratch += [pltpu.SMEM((2 * plan.capacity,), jnp.int32)]
    out_shape += [pltpu.VMEM(stacked, jnp.float32)] * 3
    out_specs += [kept] * 3
    if stage.opening:
        out_shape += [pltpu.VMEM(stacked, jnp.bfloat16), pltpu.VMEM((req_dev, 2, TILE, HD), jnp.float32)]
        out_specs += [kept] * 2
    scores = len(stage.ranks) * span * ROWS * plan.q_heads
    result = pl.pallas_call(
        functools.partial(attend_kernel, plan, stage),
        out_shape=out_shape,
        grid_spec=pltpu.PrefetchScalarGridSpec(
            num_scalar_prefetch=5,
            grid=(req_dev,),
            in_specs=specs,
            out_specs=out_specs,
            scratch_shapes=scratch,
        ),
        input_output_aliases=aliases,
        compiler_params=pltpu.CompilerParams(vmem_limit_bytes=20 << 20),
        cost_estimate=pl.CostEstimate(
            flops=4 * scores * HD,
            bytes_accessed=req_dev * ROWS * plan.q_columns * 4,
            transcendentals=scores,
        ),
        name=f"attend_{stage.step}_{stage.ranks[0]}",
    )(*operands)
    if stage.closing:
        return result[0]
    return result if stage.opening else list(result) + list(state[3:])


class Stage:
    def __init__(self, step, ranks, chunks, opening=False, closing=False):
        self.step, self.ranks, self.chunks = step, ranks, chunks
        self.opening, self.closing = opening, closing


def body(
    fresh_query,
    fresh_keys,
    fresh_values,
    store_keys,
    store_values,
    span_ids,
    span_slot,
    select_pos,
    ask_len,
):
    plan = Plan(fresh_query, fresh_keys, store_keys, span_ids, span_slot)
    store_index = lax.axis_index("store")
    ids = span_ids.reshape(-1)
    chosen = jnp.transpose(select_pos)
    steps = list(range(1, plan.stores))
    if plan.stores == 4:
        steps = [2, 1, 3]
    arrived = {}
    for step in steps + [0]:
        chunks = plan.split if step == steps[-1] else plan.chunks
        own_ids = ids
        if step == 0:
            own_ids, _ = lax.optimization_barrier((ids, first_packed))
        packed = pack(plan, step, chunks, own_ids, span_slot, chosen, store_keys, store_values)
        if step == steps[0]:
            first_packed = packed[0]
        at = 0
        for chunk in range(len(chunks)):
            for turn in range(plan.cores):
                block = packed[at]
                at += 1
                if step != 0 or turn != 0:
                    block = lax.ppermute(block, ("store", "sub"), plan.pairs(step, turn))
                arrived[(step, chunk, turn)] = block
    my_pos = lax.dynamic_slice_in_dim(select_pos, store_index * plan.req_dev, plan.req_dev, 0)
    lengths = lax.dynamic_slice_in_dim(ask_len, store_index * plan.req_dev, plan.req_dev, 0)
    asked = jnp.broadcast_to(CTX + jnp.arange(QLEN, dtype=jnp.int32), (plan.req_dev, QLEN))
    pos = jnp.concatenate([my_pos, asked], axis=1)
    pos_column = pos[:, :, None]
    pos = pos.reshape(-1)
    all_ranks = list(range(plan.capacity))
    stages = [Stage(step, all_ranks, plan.chunks) for step in [0] + steps]
    stages[0].opening = True
    if len(plan.split) > 1:
        stages[-1:] = [
            Stage(steps[-1], all_ranks[:-1], plan.split[:-1]),
            Stage(steps[-1], all_ranks[-1:], plan.split),
        ]
    stages[-1].closing = True
    state = None
    for stage in stages:
        arrays = [
            arrived[(stage.step, chunk, turn)]
            for chunk in range(len(stage.chunks))
            for turn in range(plan.cores)
        ]
        state = attend(
            plan, stage, state, arrays, (fresh_query, fresh_keys, fresh_values), ids, span_slot,
            my_pos, pos, pos_column, lengths,
        )
    return state


def solution(mesh):
    placed = (
        P(("groups", "store"), None, ("head", "sub")),
        P(("groups", "store"), None, "head"),
        P(("groups", "store"), None, "head"),
        P(("groups", "store"), "sub", "head"),
        P(("groups", "store"), "sub", "head"),
        P("groups", None),
        P("groups"),
        P("groups", None),
        P("groups"),
    )
    return jax.shard_map(
        body,
        mesh=mesh,
        in_specs=placed,
        out_specs=P(("groups", "store"), None, ("head", "sub")),
        check_vma=False,
    )
```

```python
import functools
import math

import jax
import jax.numpy as jnp
from jax import lax
from jax.experimental import pallas as pl
from jax.experimental.pallas import tpu as pltpu
from jax.sharding import PartitionSpec as P


HD = 128
GROUP = 8
SPAN = 512
NCH = 6
CTX = 3072
SEL = 464
QLEN = 64
ROWS = 528

NEGATIVE = -1e30
LIMIT = 108.0
TILE = 48
LOG_SCALE = HD ** (-0.5) * math.log2(math.e)


class Plan:
    def __init__(self, fresh_query, store_keys, span_ids):
        self.stores = lax.axis_size("store")
        self.cores = lax.axis_size("sub")
        self.req_dev = fresh_query.shape[0]
        self.ch_dev, self.half, self.kv_columns = store_keys.shape
        self.refs = self.req_dev * NCH
        self.capacity = (self.refs + self.stores - 1) // self.stores
        self.q_columns = fresh_query.shape[2]
        self.q_heads = self.q_columns // HD
        self.kv_used = max(self.q_heads // GROUP, 1)
        self.per_kv = self.q_heads // self.kv_used
        self.width = self.kv_used * HD
        self.reqs = span_ids.shape[0]
        self.source_rows = self.capacity * self.half
        self.sent_rows = self.source_rows
        self.chunks = ((0, self.sent_rows),)
        self.split = self.chunks
        if self.capacity > 1:
            first = (self.capacity - 1) * self.half
            self.split = ((0, first), (first, self.sent_rows - first))
        self.kv_block = lax.div(lax.axis_index("sub") * self.q_heads, GROUP * self.kv_used)

    def kv_start(self, core):
        return pl.multiple_of(lax.div(core * self.q_heads, GROUP) * HD, HD)

    def partner(self, store, step):
        if self.stores & (self.stores - 1) == 0:
            return store ^ step
        return lax.rem(store + step, self.stores)

    def origin(self, store, step):
        if self.stores & (self.stores - 1) == 0:
            return store ^ step
        return lax.rem(store + self.stores - step, self.stores)

    def pairs(self, step, turn):
        listed = []
        for store in range(self.stores):
            for core in range(self.cores):
                if self.stores & (self.stores - 1) == 0:
                    other = store ^ step
                else:
                    other = (store + step) % self.stores
                listed.append((store * self.cores + core, other * self.cores + (core + turn) % self.cores))
        return listed


def find_spans(plan, ids_ref, slot_ref, source, dest):
    zero = jnp.int32(0)
    places, owners, turns, live = ([zero] * plan.capacity for _ in range(4))
    seen = zero
    for turn in range(NCH):
        for request in range(plan.req_dev):
            slot = slot_ref[ids_ref[(dest * plan.req_dev + request) * NCH + turn]]
            place = slot - source * plan.ch_dev
            hit = (place >= 0) & (place < plan.ch_dev)
            for rank in range(plan.capacity):
                here = hit & (seen == rank)
                places[rank] = jnp.where(here, place, places[rank])
                owners[rank] = jnp.where(here, request, owners[rank])
                turns[rank] = jnp.where(here, turn, turns[rank])
                live[rank] = jnp.where(here, 1, live[rank])
            seen = seen + hit.astype(jnp.int32)
    return places, owners, turns, live


def live_ranks(plan, chosen_ref, dest, core, owners, turns, live):
    lane_request = lax.broadcasted_iota(jnp.int32, chosen_ref.shape, 1)
    lane = lax.broadcasted_iota(jnp.int32, (SEL, plan.half), 1)
    before = (
        lax.broadcasted_iota(jnp.int32, (plan.half, plan.half), 0)
        < lax.broadcasted_iota(jnp.int32, (plan.half, plan.half), 1)
    ).astype(jnp.bfloat16)
    sent = jnp.zeros((1, 1), jnp.float32)
    ranks = []
    for rank in range(plan.capacity):
        request = dest * plan.req_dev + owners[rank]
        column = jnp.sum(jnp.where(lane_request == request, chosen_ref[...], 0), axis=1, keepdims=True)
        base = turns[rank] * SPAN + core * plan.half
        hits = jnp.where(column - base == lane, 1.0, 0.0)
        keep = (1.0 - jnp.sum(hits, axis=0, keepdims=True)) * live[rank].astype(jnp.float32)
        ahead = jnp.dot(
            jnp.broadcast_to(keep, (16, plan.half)).astype(jnp.bfloat16), before,
            preferred_element_type=jnp.float32,
        )[:1]
        ranks.append(jnp.where(keep > 0.5, ahead + sent, -1.0))
        sent = sent + jnp.sum(keep, axis=1, keepdims=True)
    return jnp.concatenate(ranks, axis=1).astype(jnp.int32)


def selection(ranks, row_first, rows):
    wanted = lax.broadcasted_iota(jnp.int32, (rows, ranks.shape[1]), 0) + row_first
    return jnp.where(wanted == ranks, 1.0, 0.0).astype(jnp.bfloat16)


def pack_kernel(plan, step, chunks, ids_ref, slot_ref, chosen_ref, keys_ref, values_ref, *rest):
    outs, (key_rows, value_rows, sems) = rest[: -3], rest[-3:]
    store, core = lax.axis_index("store"), lax.axis_index("sub")
    dest = plan.partner(store, step)
    places, owners, turns, live = find_spans(plan, ids_ref, slot_ref, store, dest)
    copies = []
    for rank in range(plan.capacity):
        rows = pl.ds(rank * plan.half, plan.half)
        copies.append(pltpu.make_async_copy(keys_ref.at[places[rank]], key_rows.at[rows], sems.at[0, rank]))
        copies.append(pltpu.make_async_copy(values_ref.at[places[rank]], value_rows.at[rows], sems.at[1, rank]))
    for copy in copies:
        copy.start()
    ranks = live_ranks(plan, chosen_ref, dest, core, owners, turns, live)
    for copy in copies:
        copy.wait()
    for row_first, rows in tiles(plan.sent_rows):
        first = row_first // plan.half * plan.half
        select = selection(ranks[:, first:], row_first, rows)
        for turn in range(plan.cores):
            start = plan.kv_start(lax.rem(core + turn, plan.cores))
            for number, (chunk_first, chunk_rows) in enumerate(chunks):
                if chunk_first <= row_first < chunk_first + chunk_rows:
                    out = outs[number * plan.cores + turn]
                    place = slice(row_first - chunk_first, row_first - chunk_first + rows)
            for source, offset in ((key_rows, 0), (value_rows, plan.width)):
                out[place, offset : offset + plan.width] = jnp.dot(
                    select, source[first:, pl.ds(start, plan.width)], preferred_element_type=jnp.float32
                ).astype(jnp.bfloat16)


def tiles(rows, size=256):
    return [(first, min(size, rows - first)) for first in range(0, rows, size)]


def pack(plan, step, chunks, ids, slots, chosen, store_keys, store_values):
    shapes = [
        jax.ShapeDtypeStruct((rows, 2 * plan.width), jnp.bfloat16)
        for _, rows in chunks
        for _ in range(plan.cores)
    ]
    return pl.pallas_call(
        functools.partial(pack_kernel, plan, step, chunks),
        out_shape=shapes,
        grid_spec=pltpu.PrefetchScalarGridSpec(
            num_scalar_prefetch=2,
            grid=(1,),
            in_specs=[
                pl.BlockSpec(chosen.shape, lambda i, *_: (0, 0)),
                pl.BlockSpec(memory_space=pl.ANY),
                pl.BlockSpec(memory_space=pl.ANY),
            ],
            out_specs=[pl.BlockSpec(s.shape, lambda i, *_: (0, 0)) for s in shapes],
            scratch_shapes=[
                pltpu.VMEM((plan.source_rows, plan.kv_columns), jnp.bfloat16),
                pltpu.VMEM((plan.source_rows, plan.kv_columns), jnp.bfloat16),
                pltpu.SemaphoreType.DMA((2, plan.capacity)),
            ],
        ),
        cost_estimate=pl.CostEstimate(
            flops=4 * plan.source_rows**2 * plan.kv_columns,
            bytes_accessed=8 * plan.source_rows * plan.kv_columns,
            transcendentals=0,
        ),
    )(ids, slots, chosen, store_keys, store_values)


def spans_before(position_row, start):
    return jnp.sum(jnp.where(position_row < start, 1.0, 0.0), axis=1, keepdims=True)


def blend(plan, stage, table, my_pos_ref, fresh_key_ref, fresh_value_ref, streams, keys, values):
    core = lax.axis_index("sub")
    for turn in range(plan.cores):
        source_core = lax.rem(core + plan.cores - turn, plan.cores)
        offset = jnp.zeros((1, 1), jnp.float32)
        for rank in range(max(stage.ranks) + 1):
            owner, base = table[2 * rank], table[2 * rank + 1] + source_core * plan.half
            live = owner >= 0
            request = jnp.maximum(owner, 0)
            listed = my_pos_ref[pl.ds(request, 1), :]
            first = spans_before(listed, base)
            taken = spans_before(listed, base + plan.half) - first
            if rank in stage.ranks:
                at = stage.ranks.index(rank)

                @pl.when(live)
                def _(at=at, offset=offset, first=first, listed=listed, base=base, request=request):
                    token = lax.broadcasted_iota(jnp.int32, (plan.half, SEL), 0) + base
                    same = jnp.where(listed == token, 1.0, 0.0)
                    ahead = jnp.sum(jnp.where(listed < token, 1.0, 0.0), axis=1, keepdims=True)
                    chosen = jnp.sum(same, axis=1, keepdims=True)
                    row = lax.broadcasted_iota(jnp.int32, (plan.half, 1), 0).astype(jnp.float32)
                    row = row + offset - ahead + first
                    row = jnp.where(chosen > 0.5, -1.0, row).astype(jnp.int32)
                    fresh_pick = same.astype(jnp.bfloat16)
                    key = jnp.dot(fresh_pick, fresh_key_ref[request, :SEL, :], preferred_element_type=jnp.float32)
                    value = jnp.dot(fresh_pick, fresh_value_ref[request, :SEL, :], preferred_element_type=jnp.float32)
                    if len(stage.chunks) == 1 and plan.sent_rows >= plan.half + 16:
                        rows = plan.half + 16
                        below = jnp.max(offset.astype(jnp.int32)) // 16 * 16
                        below = pl.multiple_of(jnp.minimum(below, plan.sent_rows - rows), 16)
                        parts = [(below, rows, streams[turn], pl.ds(below, rows))]
                    else:
                        parts = [
                            (first_row, rows, streams[number * plan.cores + turn], slice(None))
                            for number, (first_row, rows) in enumerate(stage.chunks)
                        ]
                    for first_row, rows, stream, window in parts:
                        lane = lax.broadcasted_iota(jnp.int32, (plan.half, rows), 1) + first_row
                        pick = jnp.where(lane == row, 1.0, 0.0).astype(jnp.bfloat16)
                        both = jnp.dot(pick, stream[window, :], preferred_element_type=jnp.float32)
                        key = key + both[:, : plan.width]
                        value = value + both[:, plan.width :]
                    place = pl.ds(pl.multiple_of(source_core * plan.half, plan.half), plan.half)
                    keys[at, place, :] = key.astype(jnp.bfloat16)
                    values[at, place, :] = value.astype(jnp.bfloat16)

            offset = offset + (plan.half - taken) * live.astype(jnp.float32)


def attend_kernel(plan, stage, *refs):
    refs = list(refs)

    def take(count):
        taken = refs[:count]
        del refs[:count]
        return taken

    ids_ref, slot_ref, pos_ref, len_ref, _ = take(5)
    column_ref, my_pos_ref, fresh_key_ref, fresh_value_ref = take(4)
    if stage.opening:
        (query_in,) = take(1)
    else:
        query, sizes = take(2)
        take(3)
    streams = take(len(stage.chunks) * plan.cores)
    if stage.closing:
        (out_ref,) = take(1)
    total_ref, sums_ref, top_ref = take(3)
    if stage.opening:
        query, sizes = take(2)
    keys, values, table = take(3)
    request = pl.program_id(0)
    store = lax.axis_index("store")
    span = plan.half * plan.cores
    last = ROWS // TILE
    bunch = plan.per_kv * TILE

    @pl.when(request == 0)
    def _():
        source = plan.origin(store, stage.step)
        _, owners, turns, live = find_spans(plan, ids_ref, slot_ref, source, store)
        for rank in range(plan.capacity):
            table[2 * rank] = jnp.where(live[rank] > 0, owners[rank], -1)
            table[2 * rank + 1] = turns[rank] * SPAN
        blend(plan, stage, table, my_pos_ref, fresh_key_ref, fresh_value_ref, streams, keys, values)

    def rows_of(tile):
        return pl.ds(pl.multiple_of(tile * TILE, 16), TILE)

    def bunch_of(tile, count=1):
        return pl.ds(pl.multiple_of(tile * bunch, 16), count * bunch)

    def members():
        for kv in range(plan.kv_used):
            for member in range(plan.per_kv):
                head = kv * plan.per_kv + member
                yield kv, member, slice(head * HD, (head + 1) * HD)

    if stage.opening:
        def prepare(tile, most):
            long, low = most
            for kv, member, lanes in members():
                place = pl.ds(pl.multiple_of(tile * bunch + member * TILE, 16), TILE)
                taken = query_in[0, rows_of(tile), lanes]
                query[request, kv, place, :] = taken
                taken = taken.astype(jnp.float32)
                own = fresh_key_ref[request, rows_of(tile), kv * HD : (kv + 1) * HD].astype(jnp.float32)
                product = jnp.broadcast_to(jnp.sum(taken * own, axis=1, keepdims=True), (TILE, HD))
                top_ref[request, kv, place, :] = product
                total_ref[request, kv, place, :] = jnp.zeros((TILE, HD), jnp.float32)
                sums_ref[request, kv, place, :] = jnp.zeros((TILE, HD), jnp.float32)
                long = jnp.maximum(long, jnp.sum(jnp.abs(taken), axis=1, keepdims=True))
                low = jnp.maximum(low, -product)
            return long, low

        none = jnp.zeros((TILE, HD), jnp.float32)
        long, low = lax.fori_loop(0, last, prepare, (none, none))
        sizes[request, 0] = long
        sizes[request, 1] = low

    def masks(tile, count, width, base):
        lane = lax.broadcasted_iota(jnp.int32, (TILE, width), 1) + base
        return [lane <= column_ref[0, rows_of(tile + more), :] for more in range(count)]

    def quick(tile, count, kv, key, extended, allowed):
        rows = bunch_of(tile, count)
        scores = lax.dot_general(
            query[request, kv, rows, :], key, (((1,), (1,)), ((), ())), preferred_element_type=jnp.float32
        )
        width = key.shape[0] // HD
        powers = []
        for more in range(count):
            for member in range(plan.per_kv):
                first = more * bunch + member * TILE
                place = pl.ds(pl.multiple_of(tile * bunch + first, 16), TILE)
                shift = jnp.concatenate([top_ref[request, kv, place, :]] * width, axis=1)
                power = jnp.exp2((scores[first : first + TILE] - shift) * LOG_SCALE)
                powers.append(jnp.where(allowed[more], power, 0.0).astype(jnp.bfloat16))
        update = jnp.dot(jnp.concatenate(powers, axis=0), extended, preferred_element_type=jnp.float32)
        total_ref[request, kv, rows, :] += update[:, :HD]
        sums_ref[request, kv, rows, :] += update[:, HD:]

    def careful(tile, count, kv, key, extended, allowed):
        def one(number, unused):
            place = pl.ds(pl.multiple_of(tile * bunch + number * TILE, 16), TILE)
            scores = lax.dot_general(
                query[request, kv, place, :], key, (((1,), (1,)), ((), ())), preferred_element_type=jnp.float32
            )
            scores = jnp.where(allowed[0], scores, NEGATIVE)
            old_top = top_ref[request, kv, place, :]
            new_top = jnp.maximum(old_top, jnp.max(scores, axis=1, keepdims=True))
            shift = jnp.concatenate([new_top] * (key.shape[0] // HD), axis=1)
            powers = jnp.exp2((scores - shift) * LOG_SCALE)
            update = jnp.dot(powers.astype(jnp.bfloat16), extended, preferred_element_type=jnp.float32)
            factor = jnp.exp2((old_top - new_top) * LOG_SCALE)
            total_ref[request, kv, place, :] = total_ref[request, kv, place, :] * factor + update[:, :HD]
            sums_ref[request, kv, place, :] = sums_ref[request, kv, place, :] * factor + update[:, HD:]
            top_ref[request, kv, place, :] = new_top
            return unused

        lax.fori_loop(0, plan.per_kv, one, 0)

    def extend(value):
        return jnp.concatenate([value, jnp.ones(value.shape, jnp.bfloat16)], axis=1)

    def last_pos(tile):
        return pos_ref[request * ROWS + (tile + 1) * TILE - 1]

    def run(act, pairs):
        def span_tiles(at, base, tile, count):
            allowed = masks(tile, count, span, base)
            for kv in range(plan.kv_used):
                lanes = slice(kv * HD, (kv + 1) * HD)
                act(tile, count, kv, keys[at, :, lanes], extend(values[at, :, lanes]), allowed)

        def one_span(at, unused):
            rank = at + stage.ranks[0]
            owner, base = table[2 * rank], table[2 * rank + 1]

            @pl.when(owner == request)
            def _():
                if not pairs:
                    def step(tile, unused):
                        span_tiles(at, base, tile, 1)
                        return unused

                    lax.fori_loop(0, last, step, 0)
                    return

                @pl.when(last_pos(0) >= base)
                def _():
                    span_tiles(at, base, 0, 1)

                first = jnp.int32(0)
                for pair in range(last // 2):
                    first = first + (last_pos(2 * pair + 2) < base).astype(jnp.int32)

                def step(pair, unused):
                    span_tiles(at, base, 2 * pair + 1, 2)
                    return unused

                lax.fori_loop(first, last // 2, step, 0)

            return unused

        lax.fori_loop(0, len(stage.ranks), one_span, 0)
        if stage.opening:
            def ask(tile, unused):
                allowed = masks(tile, 1, 2 * QLEN, CTX)
                for kv in range(plan.kv_used):
                    lanes = slice(kv * HD, (kv + 1) * HD)
                    key, value = fresh_key_ref[request, SEL:, lanes], fresh_value_ref[request, SEL:, lanes]
                    key = jnp.concatenate([key, jnp.zeros_like(key)], axis=0)
                    value = jnp.concatenate([value, jnp.zeros_like(value)], axis=0)
                    act(tile, 1, kv, key, extend(value), allowed)
                return unused

            lax.fori_loop(SEL // TILE, last, ask, 0)

    greatest = jnp.max(jnp.abs(keys[...].astype(jnp.float32)))
    if stage.opening:
        greatest = jnp.maximum(greatest, jnp.max(jnp.abs(fresh_key_ref[request].astype(jnp.float32))))
    reach = (greatest * jnp.max(sizes[request, 0]) + jnp.max(sizes[request, 1])) * LOG_SCALE
    held = reach < LIMIT

    @pl.when(held)
    def _():
        run(quick, True)

    @pl.when(jnp.logical_not(held))
    def _():
        run(careful, False)

    if stage.closing:
        def finish(tile, unused):
            row = lax.broadcasted_iota(jnp.int32, (TILE, HD), 0) + tile * TILE
            live = row < SEL + len_ref[request]
            for kv, member, lanes in members():
                place = pl.ds(pl.multiple_of(tile * bunch + member * TILE, 16), TILE)
                result = total_ref[request, kv, place, :] / sums_ref[request, kv, place, :]
                out_ref[0, rows_of(tile), lanes] = jnp.where(live, result, 0.0).astype(jnp.bfloat16)
            return unused

        lax.fori_loop(0, last, finish, 0)


def attend(plan, stage, state, arrays, fresh, ids, slots, my_pos, pos, pos_column, lengths):
    fresh_query, fresh_keys, fresh_values = fresh
    req_dev = plan.req_dev
    row_block = lambda width: pl.BlockSpec((1, ROWS, width), lambda r, *_: (r, 0, 0))
    whole = lambda array: pl.BlockSpec(array.shape, lambda r, *_: (0,) * array.ndim)
    kept = pl.BlockSpec(memory_space=pltpu.VMEM)
    fresh_block = pl.BlockSpec((req_dev, ROWS, plan.width), lambda r, *s: (0, 0, s[4][0]))
    kv_block = jnp.reshape(plan.kv_block, (1,))
    operands = [ids, slots, pos, lengths, kv_block, pos_column, my_pos, fresh_keys, fresh_values]
    specs = [row_block(1), whole(my_pos), fresh_block, fresh_block]
    aliases = {}
    stacked = (req_dev, plan.kv_used, plan.q_heads // plan.kv_used * ROWS, HD)
    out_shape, out_specs = [], []
    if stage.closing:
        out_shape = [jax.ShapeDtypeStruct(fresh_query.shape, jnp.bfloat16)]
        out_specs = [row_block(plan.q_columns)]
    if stage.opening:
        operands.append(fresh_query)
        specs.append(row_block(plan.q_columns))
    else:
        aliases = {len(operands) + 2 + i: len(out_shape) + i for i in range(3)}
        operands += [state[3], state[4], *state[:3]]
        specs += [kept] * 5
    operands += arrays
    specs += [whole(a) for a in arrays]
    span = plan.half * plan.cores
    scratch = [pltpu.VMEM((len(stage.ranks), span, plan.width), jnp.bfloat16)] * 2
    scratch += [pltpu.SMEM((2 * plan.capacity,), jnp.int32)]
    out_shape += [pltpu.VMEM(stacked, jnp.float32)] * 3
    out_specs += [kept] * 3
    if stage.opening:
        out_shape += [pltpu.VMEM(stacked, jnp.bfloat16), pltpu.VMEM((req_dev, 2, TILE, HD), jnp.float32)]
        out_specs += [kept] * 2
    scores = len(stage.ranks) * span * ROWS * plan.q_heads
    result = pl.pallas_call(
        functools.partial(attend_kernel, plan, stage),
        out_shape=out_shape,
        grid_spec=pltpu.PrefetchScalarGridSpec(
            num_scalar_prefetch=5,
            grid=(req_dev,),
            in_specs=specs,
            out_specs=out_specs,
            scratch_shapes=scratch,
        ),
        input_output_aliases=aliases,
        compiler_params=pltpu.CompilerParams(vmem_limit_bytes=20 << 20),
        cost_estimate=pl.CostEstimate(
            flops=4 * scores * HD,
            bytes_accessed=req_dev * ROWS * plan.q_columns * 4,
            transcendentals=scores,
        ),
    )(*operands)
    if stage.closing:
        return result[0]
    return result if stage.opening else list(result) + list(state[3:])


class Stage:
    def __init__(self, step, ranks, chunks, opening=False, closing=False):
        self.step, self.ranks, self.chunks = step, ranks, chunks
        self.opening, self.closing = opening, closing


def body(
    fresh_query,
    fresh_keys,
    fresh_values,
    store_keys,
    store_values,
    span_ids,
    span_slot,
    select_pos,
    ask_len,
):
    plan = Plan(fresh_query, store_keys, span_ids)
    store_index = lax.axis_index("store")
    ids = span_ids.reshape(-1)
    chosen = jnp.transpose(select_pos)
    steps = list(range(1, plan.stores))
    arrived = {}
    for step in steps + [0]:
        chunks = plan.split if step == steps[-1] else plan.chunks
        own_ids = ids
        if step != steps[0]:
            own_ids, _ = lax.optimization_barrier((ids, before))
        packed = pack(plan, step, chunks, own_ids, span_slot, chosen, store_keys, store_values)
        before = packed[0]
        at = 0
        for chunk in range(len(chunks)):
            for turn in range(plan.cores):
                block = packed[at]
                at += 1
                if step != 0 or turn != 0:
                    block = lax.ppermute(block, ("store", "sub"), plan.pairs(step, turn))
                arrived[(step, chunk, turn)] = block
    my_pos = lax.dynamic_slice_in_dim(select_pos, store_index * plan.req_dev, plan.req_dev, 0)
    lengths = lax.dynamic_slice_in_dim(ask_len, store_index * plan.req_dev, plan.req_dev, 0)
    asked = jnp.broadcast_to(CTX + jnp.arange(QLEN, dtype=jnp.int32), (plan.req_dev, QLEN))
    pos = jnp.concatenate([my_pos, asked], axis=1)
    pos_column = pos[:, :, None]
    pos = pos.reshape(-1)
    all_ranks = list(range(plan.capacity))
    stages = [Stage(step, all_ranks, plan.chunks) for step in [0] + steps]
    stages[0].opening = True
    if len(plan.split) > 1:
        stages[-1:] = [
            Stage(steps[-1], all_ranks[:-1], plan.split[:-1]),
            Stage(steps[-1], all_ranks[-1:], plan.split),
        ]
    stages[-1].closing = True
    state = None
    for stage in stages:
        arrays = [
            arrived[(stage.step, chunk, turn)]
            for chunk in range(len(stage.chunks))
            for turn in range(plan.cores)
        ]
        state = attend(
            plan, stage, state, arrays, (fresh_query, fresh_keys, fresh_values), ids, span_slot,
            my_pos, pos, pos_column, lengths,
        )
    return state


def solution(mesh):
    placed = (
        P(("groups", "store"), None, ("head", "sub")),
        P(("groups", "store"), None, "head"),
        P(("groups", "store"), None, "head"),
        P(("groups", "store"), "sub", "head"),
        P(("groups", "store"), "sub", "head"),
        P("groups", None),
        P("groups"),
        P("groups", None),
        P("groups"),
    )
    return jax.shard_map(
        body,
        mesh=mesh,
        in_specs=placed,
        out_specs=P(("groups", "store"), None, ("head", "sub")),
        check_vma=False,
    )
```

```python
import functools
import math

import jax
import jax.numpy as jnp
from jax import lax
from jax.experimental import pallas as pl
from jax.experimental.pallas import tpu as pltpu
from jax.sharding import PartitionSpec as P


HD = 128
GROUP = 8
SPAN = 512
NCH = 6
CTX = 3072
SEL = 464
QLEN = 64
ROWS = 528

NEGATIVE = -1e30
LIMIT = 108.0
TILE = 48
LOG_SCALE = HD ** (-0.5) * math.log2(math.e)


class Plan:
    def __init__(self, fresh_query, store_keys, span_ids):
        self.stores = lax.axis_size("store")
        self.cores = lax.axis_size("sub")
        self.req_dev = fresh_query.shape[0]
        self.ch_dev, self.half, self.kv_columns = store_keys.shape
        self.refs = self.req_dev * NCH
        self.capacity = (self.refs + self.stores - 1) // self.stores
        self.q_columns = fresh_query.shape[2]
        self.q_heads = self.q_columns // HD
        self.kv_used = max(self.q_heads // GROUP, 1)
        self.per_kv = self.q_heads // self.kv_used
        self.width = self.kv_used * HD
        self.reqs = span_ids.shape[0]
        self.source_rows = self.capacity * self.half
        self.sent_rows = self.source_rows
        if self.capacity > 1:
            part = SEL / CTX
            likely = self.source_rows * (1 - part) + 3.6 * math.sqrt(self.source_rows * part * (1 - part))
            likely = -(-math.ceil(likely) // 16) * 16
            if (self.capacity - 1) * self.half < likely < self.source_rows:
                self.sent_rows = likely
        self.left_rows = self.source_rows - self.sent_rows

        self.kv_block = lax.div(lax.axis_index("sub") * self.q_heads, GROUP * self.kv_used)

    def chunks(self, step):
        edges = [0, self.sent_rows]
        if step == 0:
            edges = [0, self.source_rows]
        elif step == self.stores - 1:
            edges = [rank * self.half for rank in range(self.capacity)] + [self.sent_rows]
        elif step == self.stores - 2 and self.capacity > 1:
            edges = [0, (self.capacity - 1) * self.half, self.sent_rows]
        return [(first, end - first) for first, end in zip(edges[:-1], edges[1:])]

    def kv_start(self, core):
        return pl.multiple_of(lax.div(core * self.q_heads, GROUP) * HD, HD)

    def partner(self, store, step):
        if self.stores & (self.stores - 1) == 0:
            return store ^ step
        return lax.rem(store + step, self.stores)

    def origin(self, store, step):
        if self.stores & (self.stores - 1) == 0:
            return store ^ step
        return lax.rem(store + self.stores - step, self.stores)

    def pairs(self, step, turn):
        listed = []
        for store in range(self.stores):
            for core in range(self.cores):
                if self.stores & (self.stores - 1) == 0:
                    other = store ^ step
                else:
                    other = (store + step) % self.stores
                listed.append((store * self.cores + core, other * self.cores + (core + turn) % self.cores))
        return listed


def find_spans(plan, ids_ref, slot_ref, source, dest):
    zero = jnp.int32(0)
    places, owners, turns, live = ([zero] * plan.capacity for _ in range(4))
    seen = zero
    for turn in range(NCH):
        for request in range(plan.req_dev):
            slot = slot_ref[ids_ref[(dest * plan.req_dev + request) * NCH + turn]]
            place = slot - source * plan.ch_dev
            hit = (place >= 0) & (place < plan.ch_dev)
            for rank in range(plan.capacity):
                here = hit & (seen == rank)
                places[rank] = jnp.where(here, place, places[rank])
                owners[rank] = jnp.where(here, request, owners[rank])
                turns[rank] = jnp.where(here, turn, turns[rank])
                live[rank] = jnp.where(here, 1, live[rank])
            seen = seen + hit.astype(jnp.int32)
    return places, owners, turns, live


def live_ranks(plan, chosen_ref, dest, core, owners, turns, live):
    lane_request = lax.broadcasted_iota(jnp.int32, chosen_ref.shape, 1)
    lane = lax.broadcasted_iota(jnp.int32, (SEL, plan.half), 1)
    before = (
        lax.broadcasted_iota(jnp.int32, (plan.half, plan.half), 0)
        < lax.broadcasted_iota(jnp.int32, (plan.half, plan.half), 1)
    ).astype(jnp.bfloat16)
    sent = jnp.zeros((1, 1), jnp.float32)
    ranks = []
    for rank in range(plan.capacity):
        request = dest * plan.req_dev + owners[rank]
        column = jnp.sum(jnp.where(lane_request == request, chosen_ref[...], 0), axis=1, keepdims=True)
        base = turns[rank] * SPAN + core * plan.half
        hits = jnp.where(column - base == lane, 1.0, 0.0)
        keep = (1.0 - jnp.sum(hits, axis=0, keepdims=True)) * live[rank].astype(jnp.float32)
        ahead = jnp.dot(
            jnp.broadcast_to(keep, (16, plan.half)).astype(jnp.bfloat16), before,
            preferred_element_type=jnp.float32,
        )[:1]
        ranks.append(jnp.where(keep > 0.5, ahead + sent, -1.0))
        sent = sent + jnp.sum(keep, axis=1, keepdims=True)
    return jnp.concatenate(ranks, axis=1).astype(jnp.int32)


def selection(ranks, row_first, rows):
    wanted = lax.broadcasted_iota(jnp.int32, (rows, ranks.shape[1]), 0) + row_first
    return jnp.where(wanted == ranks, 1.0, 0.0).astype(jnp.bfloat16)


def pack_kernel(plan, step, chunks, ids_ref, slot_ref, chosen_ref, keys_ref, values_ref, *rest):
    outs, (key_rows, value_rows, sems) = rest[: -3], rest[-3:]
    store, core = lax.axis_index("store"), lax.axis_index("sub")
    dest = plan.partner(store, step)
    places, owners, turns, live = find_spans(plan, ids_ref, slot_ref, store, dest)
    copies = []
    for rank in range(plan.capacity):
        rows = pl.ds(rank * plan.half, plan.half)
        copies.append(pltpu.make_async_copy(keys_ref.at[places[rank]], key_rows.at[rows], sems.at[0, rank]))
        copies.append(pltpu.make_async_copy(values_ref.at[places[rank]], value_rows.at[rows], sems.at[1, rank]))
    for copy in copies:
        copy.start()
    ranks = live_ranks(plan, chosen_ref, dest, core, owners, turns, live)
    for copy in copies:
        copy.wait()
    for row_first, rows in [tile for chunk in chunks for tile in tiles(*chunk)]:
        first = row_first // plan.half * plan.half
        select = selection(ranks[:, first:], row_first, rows)
        for turn in range(plan.cores):
            start = plan.kv_start(lax.rem(core + turn, plan.cores))
            for number, (chunk_first, chunk_rows) in enumerate(chunks):
                if chunk_first <= row_first < chunk_first + chunk_rows:
                    out = outs[number * plan.cores + turn]
                    place = slice(row_first - chunk_first, row_first - chunk_first + rows)
            for source, offset in ((key_rows, 0), (value_rows, plan.width)):
                out[place, offset : offset + plan.width] = jnp.dot(
                    select, source[first:, pl.ds(start, plan.width)], preferred_element_type=jnp.float32
                ).astype(jnp.bfloat16)


def tiles(start, rows, size=256):
    return [(start + first, min(size, rows - first)) for first in range(0, rows, size)]


def pack(plan, step, chunks, ids, slots, chosen, store_keys, store_values):
    shapes = [
        jax.ShapeDtypeStruct((rows, 2 * plan.width), jnp.bfloat16)
        for _, rows in chunks
        for _ in range(plan.cores)
    ]
    return pl.pallas_call(
        functools.partial(pack_kernel, plan, step, chunks),
        out_shape=shapes,
        grid_spec=pltpu.PrefetchScalarGridSpec(
            num_scalar_prefetch=2,
            grid=(1,),
            in_specs=[
                pl.BlockSpec(chosen.shape, lambda i, *_: (0, 0)),
                pl.BlockSpec(memory_space=pl.ANY),
                pl.BlockSpec(memory_space=pl.ANY),
            ],
            out_specs=[pl.BlockSpec(s.shape, lambda i, *_: (0, 0)) for s in shapes],
            scratch_shapes=[
                pltpu.VMEM((plan.source_rows, plan.kv_columns), jnp.bfloat16),
                pltpu.VMEM((plan.source_rows, plan.kv_columns), jnp.bfloat16),
                pltpu.SemaphoreType.DMA((2, plan.capacity)),
            ],
        ),
        cost_estimate=pl.CostEstimate(
            flops=4 * plan.source_rows**2 * plan.kv_columns,
            bytes_accessed=8 * plan.source_rows * plan.kv_columns,
            transcendentals=0,
        ),
    )(ids, slots, chosen, store_keys, store_values)


def spans_before(position_row, start):
    return jnp.sum(jnp.where(position_row < start, 1.0, 0.0), axis=1, keepdims=True)


def blend(plan, stage, table, left_ref, my_pos_ref, fresh_key_ref, fresh_value_ref, joined, keys, values):
    core = lax.axis_index("sub")
    held = sum(rows for _, rows in stage.chunks)
    rows = min(plan.half + 16, held)

    def one_turn(turn, unused):
        source_core = lax.rem(core + plan.cores - turn, plan.cores)

        def one_rank(rank, offset):
            owner, base = table[2 * rank], table[2 * rank + 1] + source_core * plan.half
            live = owner >= 0
            request = jnp.maximum(owner, 0)
            listed = my_pos_ref[pl.ds(request, 1), :]
            first = spans_before(listed, base)
            taken = spans_before(listed, base + plan.half) - first

            @pl.when(live & (rank >= stage.ranks[0]))
            def _():
                token = lax.broadcasted_iota(jnp.int32, (plan.half, SEL), 0) + base
                same = jnp.where(listed == token, 1.0, 0.0)
                ahead = jnp.sum(jnp.where(listed < token, 1.0, 0.0), axis=1, keepdims=True)
                chosen = jnp.sum(same, axis=1, keepdims=True)
                row = lax.broadcasted_iota(jnp.int32, (plan.half, 1), 0).astype(jnp.float32)
                row = row + offset - ahead + first
                row = jnp.where(chosen > 0.5, -1.0, row).astype(jnp.int32)
                fresh_pick = same.astype(jnp.bfloat16)
                key = jnp.dot(fresh_pick, fresh_key_ref[request, :SEL, :], preferred_element_type=jnp.float32)
                value = jnp.dot(fresh_pick, fresh_value_ref[request, :SEL, :], preferred_element_type=jnp.float32)
                below = jnp.max(offset.astype(jnp.int32)) // 16 * 16
                below = pl.multiple_of(jnp.minimum(below, held - rows), 16)
                lane = lax.broadcasted_iota(jnp.int32, (plan.half, rows), 1) + below
                pick = jnp.where(lane == row, 1.0, 0.0).astype(jnp.bfloat16)
                both = jnp.dot(pick, joined[turn, pl.ds(below, rows), :], preferred_element_type=jnp.float32)
                at = rank - stage.ranks[0]
                place = pl.ds(pl.multiple_of(source_core * plan.half, plan.half), plan.half)
                keys[at, place, :] = (key + both[:, : plan.width]).astype(jnp.bfloat16)
                values[at, place, :] = (value + both[:, plan.width :]).astype(jnp.bfloat16)
                if stage.left:
                    @pl.when(left_ref[0] > 0)
                    def _():
                        over = lax.broadcasted_iota(jnp.int32, (plan.half, plan.left_rows), 1) + plan.sent_rows
                        extra = jnp.where(over == row, 1.0, 0.0).astype(jnp.bfloat16)
                        more = jnp.dot(extra, joined[turn, held:, :], preferred_element_type=jnp.float32)
                        more = more.astype(jnp.bfloat16)
                        keys[at, place, :] += more[:, : plan.width]
                        values[at, place, :] += more[:, plan.width :]

            return offset + (plan.half - taken) * live.astype(jnp.float32)

        lax.fori_loop(0, stage.ranks[-1] + 1, one_rank, jnp.zeros((1, 1), jnp.float32))
        return unused

    lax.fori_loop(0, plan.cores, one_turn, 0)


def attend_kernel(plan, stage, *refs):
    refs = list(refs)

    def take(count):
        taken = refs[:count]
        del refs[:count]
        return taken

    ids_ref, slot_ref, pos_ref, len_ref, _, left_ref = take(6)
    column_ref, my_pos_ref, fresh_key_ref, fresh_value_ref = take(4)
    if stage.opening:
        (query_in,) = take(1)
    else:
        query, sizes = take(2)
        take(3)
    streams = take((len(stage.chunks) + stage.left) * plan.cores)
    if stage.closing:
        (out_ref,) = take(1)
    total_ref, sums_ref, top_ref = take(3)
    if stage.opening:
        query, sizes = take(2)
    keys, values, joined, table = take(4)
    request = pl.program_id(0)
    store = lax.axis_index("store")
    span = plan.half * plan.cores
    last = ROWS // TILE
    bunch = plan.per_kv * TILE

    @pl.when(request == 0)
    def _():
        source = plan.origin(store, stage.step)
        _, owners, turns, live = find_spans(plan, ids_ref, slot_ref, source, store)
        for rank in range(plan.capacity):
            table[2 * rank] = jnp.where(live[rank] > 0, owners[rank], -1)
            table[2 * rank + 1] = turns[rank] * SPAN
        at = 0
        for number in range(len(stage.chunks) + stage.left):
            rows = streams[number * plan.cores].shape[0]
            for turn in range(plan.cores):
                joined[turn, at : at + rows, :] = streams[number * plan.cores + turn][...]
            at += rows
        blend(plan, stage, table, left_ref, my_pos_ref, fresh_key_ref, fresh_value_ref, joined, keys, values)

    def rows_of(tile):
        return pl.ds(pl.multiple_of(tile * TILE, 16), TILE)

    def bunch_of(tile, count=1):
        return pl.ds(pl.multiple_of(tile * bunch, 16), count * bunch)

    def members():
        for kv in range(plan.kv_used):
            for member in range(plan.per_kv):
                head = kv * plan.per_kv + member
                yield kv, member, slice(head * HD, (head + 1) * HD)

    if stage.opening:
        def prepare(tile, most):
            long, low = most
            for kv, member, lanes in members():
                place = pl.ds(pl.multiple_of(tile * bunch + member * TILE, 16), TILE)
                taken = query_in[0, rows_of(tile), lanes]
                query[request, kv, place, :] = taken
                taken = taken.astype(jnp.float32)
                own = fresh_key_ref[request, rows_of(tile), kv * HD : (kv + 1) * HD].astype(jnp.float32)
                product = jnp.broadcast_to(jnp.sum(taken * own, axis=1, keepdims=True), (TILE, HD))
                top_ref[request, kv, place, :] = product
                total_ref[request, kv, place, :] = jnp.zeros((TILE, HD), jnp.float32)
                sums_ref[request, kv, place, :] = jnp.zeros((TILE, HD), jnp.float32)
                long = jnp.maximum(long, jnp.sum(jnp.abs(taken), axis=1, keepdims=True))
                low = jnp.maximum(low, -product)
            return long, low

        none = jnp.zeros((TILE, HD), jnp.float32)
        long, low = lax.fori_loop(0, last, prepare, (none, none))
        sizes[request, 0] = long
        sizes[request, 1] = low

    def masks(tile, count, width, base):
        lane = lax.broadcasted_iota(jnp.int32, (TILE, width), 1) + base
        return [lane <= column_ref[0, rows_of(tile + more), :] for more in range(count)]

    def quick(tile, count, kv, key, extended, allowed):
        rows = bunch_of(tile, count)
        scores = lax.dot_general(
            query[request, kv, rows, :], key, (((1,), (1,)), ((), ())), preferred_element_type=jnp.float32
        )
        width = key.shape[0] // HD
        powers = []
        for more in range(count):
            for member in range(plan.per_kv):
                first = more * bunch + member * TILE
                place = pl.ds(pl.multiple_of(tile * bunch + first, 16), TILE)
                shift = jnp.concatenate([top_ref[request, kv, place, :]] * width, axis=1)
                power = jnp.exp2((scores[first : first + TILE] - shift) * LOG_SCALE)
                powers.append(jnp.where(allowed[more], power, 0.0).astype(jnp.bfloat16))
        update = jnp.dot(jnp.concatenate(powers, axis=0), extended, preferred_element_type=jnp.float32)
        total_ref[request, kv, rows, :] += update[:, :HD]
        sums_ref[request, kv, rows, :] += update[:, HD:]

    def careful(tile, count, kv, key, extended, allowed):
        def one(number, unused):
            place = pl.ds(pl.multiple_of(tile * bunch + number * TILE, 16), TILE)
            scores = lax.dot_general(
                query[request, kv, place, :], key, (((1,), (1,)), ((), ())), preferred_element_type=jnp.float32
            )
            scores = jnp.where(allowed[0], scores, NEGATIVE)
            old_top = top_ref[request, kv, place, :]
            new_top = jnp.maximum(old_top, jnp.max(scores, axis=1, keepdims=True))
            shift = jnp.concatenate([new_top] * (key.shape[0] // HD), axis=1)
            powers = jnp.exp2((scores - shift) * LOG_SCALE)
            update = jnp.dot(powers.astype(jnp.bfloat16), extended, preferred_element_type=jnp.float32)
            factor = jnp.exp2((old_top - new_top) * LOG_SCALE)
            total_ref[request, kv, place, :] = total_ref[request, kv, place, :] * factor + update[:, :HD]
            sums_ref[request, kv, place, :] = sums_ref[request, kv, place, :] * factor + update[:, HD:]
            top_ref[request, kv, place, :] = new_top
            return unused

        lax.fori_loop(0, plan.per_kv, one, 0)

    def extend(value):
        return jnp.concatenate([value, jnp.ones(value.shape, jnp.bfloat16)], axis=1)

    def last_pos(tile):
        return pos_ref[request * ROWS + (tile + 1) * TILE - 1]

    def run(act, pairs):
        def span_tiles(at, base, tile, count):
            allowed = masks(tile, count, span, base)
            for kv in range(plan.kv_used):
                lanes = slice(kv * HD, (kv + 1) * HD)
                act(tile, count, kv, keys[at, :, lanes], extend(values[at, :, lanes]), allowed)

        def one_span(at, unused):
            rank = at + stage.ranks[0]
            owner, base = table[2 * rank], table[2 * rank + 1]

            @pl.when(owner == request)
            def _():
                if not pairs:
                    def step(tile, unused):
                        span_tiles(at, base, tile, 1)
                        return unused

                    lax.fori_loop(0, last, step, 0)
                    return

                @pl.when(last_pos(0) >= base)
                def _():
                    span_tiles(at, base, 0, 1)

                first = jnp.int32(0)
                for pair in range(last // 2):
                    first = first + (last_pos(2 * pair + 2) < base).astype(jnp.int32)

                def step(pair, unused):
                    span_tiles(at, base, 2 * pair + 1, 2)
                    return unused

                lax.fori_loop(first, last // 2, step, 0)

            return unused

        lax.fori_loop(0, len(stage.ranks), one_span, 0)
        if stage.opening:
            def ask(tile, unused):
                allowed = masks(tile, 1, 2 * QLEN, CTX)
                for kv in range(plan.kv_used):
                    lanes = slice(kv * HD, (kv + 1) * HD)
                    key, value = fresh_key_ref[request, SEL:, lanes], fresh_value_ref[request, SEL:, lanes]
                    key = jnp.concatenate([key, jnp.zeros_like(key)], axis=0)
                    value = jnp.concatenate([value, jnp.zeros_like(value)], axis=0)
                    act(tile, 1, kv, key, extend(value), allowed)
                return unused

            lax.fori_loop(SEL // TILE, last, ask, 0)

    greatest = jnp.max(jnp.abs(keys[...].astype(jnp.float32)))
    if stage.opening:
        greatest = jnp.maximum(greatest, jnp.max(jnp.abs(fresh_key_ref[request].astype(jnp.float32))))
    reach = (greatest * jnp.max(sizes[request, 0]) + jnp.max(sizes[request, 1])) * LOG_SCALE
    held = reach < LIMIT

    @pl.when(held)
    def _():
        run(quick, True)

    @pl.when(jnp.logical_not(held))
    def _():
        run(careful, False)

    if stage.closing:
        def finish(tile, unused):
            row = lax.broadcasted_iota(jnp.int32, (TILE, HD), 0) + tile * TILE
            live = row < SEL + len_ref[request]
            for kv, member, lanes in members():
                place = pl.ds(pl.multiple_of(tile * bunch + member * TILE, 16), TILE)
                result = total_ref[request, kv, place, :] / sums_ref[request, kv, place, :]
                out_ref[0, rows_of(tile), lanes] = jnp.where(live, result, 0.0).astype(jnp.bfloat16)
            return unused

        lax.fori_loop(0, last, finish, 0)


def attend(plan, stage, state, arrays, fresh, ids, slots, my_pos, pos, pos_column, lengths, left_over):
    fresh_query, fresh_keys, fresh_values = fresh
    req_dev = plan.req_dev
    row_block = lambda width: pl.BlockSpec((1, ROWS, width), lambda r, *_: (r, 0, 0))
    whole = lambda array: pl.BlockSpec(array.shape, lambda r, *_: (0,) * array.ndim)
    kept = pl.BlockSpec(memory_space=pltpu.VMEM)
    fresh_block = pl.BlockSpec((req_dev, ROWS, plan.width), lambda r, *s: (0, 0, s[4][0]))
    kv_block = jnp.reshape(plan.kv_block, (1,))
    operands = [ids, slots, pos, lengths, kv_block, left_over, pos_column, my_pos, fresh_keys, fresh_values]
    specs = [row_block(1), whole(my_pos), fresh_block, fresh_block]
    aliases = {}
    stacked = (req_dev, plan.kv_used, plan.q_heads // plan.kv_used * ROWS, HD)
    out_shape, out_specs = [], []
    if stage.closing:
        out_shape = [jax.ShapeDtypeStruct(fresh_query.shape, jnp.bfloat16)]
        out_specs = [row_block(plan.q_columns)]
    if stage.opening:
        operands.append(fresh_query)
        specs.append(row_block(plan.q_columns))
    else:
        aliases = {len(operands) + 2 + i: len(out_shape) + i for i in range(3)}
        operands += [state[3], state[4], *state[:3]]
        specs += [kept] * 5
    operands += arrays
    specs += [whole(a) for a in arrays]
    span = plan.half * plan.cores
    scratch = [pltpu.VMEM((len(stage.ranks), span, plan.width), jnp.bfloat16)] * 2
    joined_rows = sum(array.shape[0] for array in arrays) // plan.cores
    scratch += [pltpu.VMEM((plan.cores, joined_rows, 2 * plan.width), jnp.bfloat16)]
    scratch += [pltpu.SMEM((2 * plan.capacity,), jnp.int32)]
    out_shape += [pltpu.VMEM(stacked, jnp.float32)] * 3
    out_specs += [kept] * 3
    if stage.opening:
        out_shape += [pltpu.VMEM(stacked, jnp.bfloat16), pltpu.VMEM((req_dev, 2, TILE, HD), jnp.float32)]
        out_specs += [kept] * 2
    scores = len(stage.ranks) * span * ROWS * plan.q_heads
    result = pl.pallas_call(
        functools.partial(attend_kernel, plan, stage),
        out_shape=out_shape,
        grid_spec=pltpu.PrefetchScalarGridSpec(
            num_scalar_prefetch=6,
            grid=(req_dev,),
            in_specs=specs,
            out_specs=out_specs,
            scratch_shapes=scratch,
        ),
        input_output_aliases=aliases,
        compiler_params=pltpu.CompilerParams(vmem_limit_bytes=20 << 20),
        cost_estimate=pl.CostEstimate(
            flops=4 * scores * HD,
            bytes_accessed=req_dev * ROWS * plan.q_columns * 4,
            transcendentals=scores,
        ),
    )(*operands)
    if stage.closing:
        return result[0]
    return result if stage.opening else list(result) + list(state[3:])


class Stage:
    def __init__(self, step, ranks, chunks, left):
        self.step, self.ranks, self.chunks, self.left = step, ranks, chunks, left
        self.opening = self.closing = False


def most_live(plan, span_ids, span_slot, select_pos):
    halves = CTX // plan.half
    listed = (select_pos // plan.half)[:, :, None] == jnp.arange(halves, dtype=jnp.int32)
    live = plan.half - jnp.sum(listed.astype(jnp.int32), axis=1)
    spans = span_ids.reshape(plan.stores, plan.refs)
    known = spans[:, :, None] == jnp.arange(span_slot.shape[0], dtype=jnp.int32)
    owner = jnp.sum(jnp.where(known, span_slot // plan.ch_dev, 0), axis=2)
    live = live.reshape(plan.stores, plan.refs, plan.cores)
    theirs = owner[:, :, None] == jnp.arange(plan.stores, dtype=jnp.int32)
    counts = jnp.sum(jnp.where(theirs[..., None], live[:, :, None, :], 0), axis=1)
    most = jnp.max(counts).reshape(1)
    groups = lax.axis_size("groups")
    others = [
        lax.ppermute(most, "groups", [(g, (g + turn) % groups) for g in range(groups)])
        for turn in range(1, groups)
    ]
    for other in others:
        most = jnp.maximum(most, other)
    return most


def body(
    fresh_query,
    fresh_keys,
    fresh_values,
    store_keys,
    store_values,
    span_ids,
    span_slot,
    select_pos,
    ask_len,
):
    plan = Plan(fresh_query, store_keys, span_ids)
    store_index = lax.axis_index("store")
    ids = span_ids.reshape(-1)
    chosen = jnp.transpose(select_pos)
    steps = list(range(1, plan.stores))
    arrived = {}
    for step in steps + [0]:
        chunks = plan.chunks(step)
        own_ids = ids
        if step != steps[0]:
            own_ids, _ = lax.optimization_barrier((ids, before))
        packed = pack(plan, step, chunks, own_ids, span_slot, chosen, store_keys, store_values)
        before = packed[0]
        at = 0
        for chunk in range(len(chunks)):
            for turn in range(plan.cores):
                block = packed[at]
                at += 1
                if step != 0 or turn != 0:
                    block = lax.ppermute(block, ("store", "sub"), plan.pairs(step, turn))
                arrived[(step, chunk, turn)] = block
    left, left_over = {}, jnp.zeros((1,), jnp.int32)
    if plan.left_rows:
        most = most_live(plan, span_ids, span_slot, select_pos)
        left_over = (most > plan.sent_rows).astype(jnp.int32)

        def send_left():
            blocks = []
            for step in steps:
                rest = pack(
                    plan, step, [(plan.sent_rows, plan.left_rows)], ids, span_slot, chosen, store_keys, store_values
                )
                for turn in range(plan.cores):
                    blocks.append(lax.ppermute(rest[turn], ("store", "sub"), plan.pairs(step, turn)))
            return tuple(blocks)

        def nothing():
            return tuple(
                jnp.zeros((plan.left_rows, 2 * plan.width), jnp.bfloat16) for _ in steps for _ in range(plan.cores)
            )

        blocks = lax.cond(left_over[0] > 0, send_left, nothing)
        for number, step in enumerate(steps):
            left[step] = list(blocks[number * plan.cores : (number + 1) * plan.cores])
    my_pos = lax.dynamic_slice_in_dim(select_pos, store_index * plan.req_dev, plan.req_dev, 0)
    lengths = lax.dynamic_slice_in_dim(ask_len, store_index * plan.req_dev, plan.req_dev, 0)
    asked = jnp.broadcast_to(CTX + jnp.arange(QLEN, dtype=jnp.int32), (plan.req_dev, QLEN))
    pos = jnp.concatenate([my_pos, asked], axis=1)
    pos_column = pos[:, :, None]
    pos = pos.reshape(-1)
    all_ranks = list(range(plan.capacity))
    stages = []
    for step in [0] + steps:
        chunks = plan.chunks(step)
        groups = [all_ranks]
        if len(chunks) == plan.capacity:
            groups = [[rank] for rank in all_ranks]
        elif len(chunks) == 2:
            groups = [all_ranks[:-1], all_ranks[-1:]]
        for number, ranks in enumerate(groups):
            remains = step != 0 and plan.left_rows > 0 and ranks[-1] == all_ranks[-1]
            stages.append(Stage(step, ranks, chunks[: number + 1], int(remains)))
    stages[0].opening = True
    stages[-1].closing = True
    state = None
    for stage in stages:
        arrays = [
            arrived[(stage.step, chunk, turn)]
            for chunk in range(len(stage.chunks))
            for turn in range(plan.cores)
        ]
        if stage.left:
            arrays += left[stage.step]
        state = attend(
            plan, stage, state, arrays, (fresh_query, fresh_keys, fresh_values), ids, span_slot,
            my_pos, pos, pos_column, lengths, left_over,
        )
    return state


def solution(mesh):
    placed = (
        P(("groups", "store"), None, ("head", "sub")),
        P(("groups", "store"), None, "head"),
        P(("groups", "store"), None, "head"),
        P(("groups", "store"), "sub", "head"),
        P(("groups", "store"), "sub", "head"),
        P("groups", None),
        P("groups"),
        P("groups", None),
        P("groups"),
    )
    return jax.shard_map(
        body,
        mesh=mesh,
        in_specs=placed,
        out_specs=P(("groups", "store"), None, ("head", "sub")),
        check_vma=False,
    )
```

```python
import functools
import math

import jax
import jax.numpy as jnp
from jax import lax
from jax.experimental import pallas as pl
from jax.experimental.pallas import tpu as pltpu
from jax.sharding import PartitionSpec as P


HD = 128
GROUP = 8
SPAN = 512
NCH = 6
CTX = 3072
SEL = 464
QLEN = 64
ROWS = 528

NEGATIVE = -1e30
LIMIT = 108.0
TILE = 48
LOG_SCALE = HD ** (-0.5) * math.log2(math.e)


class Plan:
    def __init__(self, fresh_query, store_keys, span_ids):
        self.stores = lax.axis_size("store")
        self.cores = lax.axis_size("sub")
        self.req_dev = fresh_query.shape[0]
        self.ch_dev, self.half, self.kv_columns = store_keys.shape
        self.refs = self.req_dev * NCH
        self.capacity = (self.refs + self.stores - 1) // self.stores
        self.q_columns = fresh_query.shape[2]
        self.q_heads = self.q_columns // HD
        self.kv_used = max(self.q_heads // GROUP, 1)
        self.per_kv = self.q_heads // self.kv_used
        self.width = self.kv_used * HD
        self.reqs = span_ids.shape[0]
        self.source_rows = self.capacity * self.half
        self.sent_rows = self.source_rows
        if self.capacity > 1:
            part = SEL / CTX
            likely = self.source_rows * (1 - part) + 3.6 * math.sqrt(self.source_rows * part * (1 - part))
            likely = -(-math.ceil(likely) // 16) * 16
            if (self.capacity - 1) * self.half < likely < self.source_rows:
                self.sent_rows = likely
        self.left_rows = self.source_rows - self.sent_rows

        self.kv_block = lax.div(lax.axis_index("sub") * self.q_heads, GROUP * self.kv_used)

    def chunks(self, step):
        edges = [0, self.sent_rows]
        if step == 0:
            edges = [0, self.source_rows]
        elif step == self.stores - 1:
            edges = [rank * self.half for rank in range(self.capacity)] + [self.sent_rows]
        elif step == self.stores - 2 and self.capacity > 1:
            edges = [0, (self.capacity - 1) * self.half, self.sent_rows]
        return [(first, end - first) for first, end in zip(edges[:-1], edges[1:])]

    def kv_start(self, core):
        return pl.multiple_of(lax.div(core * self.q_heads, GROUP) * HD, HD)

    def partner(self, store, step):
        if self.stores & (self.stores - 1) == 0:
            return store ^ step
        return lax.rem(store + step, self.stores)

    def origin(self, store, step):
        if self.stores & (self.stores - 1) == 0:
            return store ^ step
        return lax.rem(store + self.stores - step, self.stores)

    def pairs(self, step, turn):
        listed = []
        for store in range(self.stores):
            for core in range(self.cores):
                if self.stores & (self.stores - 1) == 0:
                    other = store ^ step
                else:
                    other = (store + step) % self.stores
                listed.append((store * self.cores + core, other * self.cores + (core + turn) % self.cores))
        return listed


def find_spans(plan, ids_ref, slot_ref, source, dest):
    zero = jnp.int32(0)
    places, owners, turns, live = ([zero] * plan.capacity for _ in range(4))
    seen = zero
    for turn in range(NCH):
        for request in range(plan.req_dev):
            slot = slot_ref[ids_ref[(dest * plan.req_dev + request) * NCH + turn]]
            place = slot - source * plan.ch_dev
            hit = (place >= 0) & (place < plan.ch_dev)
            for rank in range(plan.capacity):
                here = hit & (seen == rank)
                places[rank] = jnp.where(here, place, places[rank])
                owners[rank] = jnp.where(here, request, owners[rank])
                turns[rank] = jnp.where(here, turn, turns[rank])
                live[rank] = jnp.where(here, 1, live[rank])
            seen = seen + hit.astype(jnp.int32)
    return places, owners, turns, live


def live_ranks(plan, chosen_ref, dest, core, owners, turns, live):
    lane_request = lax.broadcasted_iota(jnp.int32, chosen_ref.shape, 1)
    lane = lax.broadcasted_iota(jnp.int32, (SEL, plan.half), 1)
    before = (
        lax.broadcasted_iota(jnp.int32, (plan.half, plan.half), 0)
        < lax.broadcasted_iota(jnp.int32, (plan.half, plan.half), 1)
    ).astype(jnp.bfloat16)
    sent = jnp.zeros((1, 1), jnp.float32)
    ranks = []
    for rank in range(plan.capacity):
        request = dest * plan.req_dev + owners[rank]
        column = jnp.sum(jnp.where(lane_request == request, chosen_ref[...], 0), axis=1, keepdims=True)
        base = turns[rank] * SPAN + core * plan.half
        hits = jnp.where(column - base == lane, 1.0, 0.0)
        keep = (1.0 - jnp.sum(hits, axis=0, keepdims=True)) * live[rank].astype(jnp.float32)
        ahead = jnp.dot(
            jnp.broadcast_to(keep, (16, plan.half)).astype(jnp.bfloat16), before,
            preferred_element_type=jnp.float32,
        )[:1]
        ranks.append(jnp.where(keep > 0.5, ahead + sent, -1.0))
        sent = sent + jnp.sum(keep, axis=1, keepdims=True)
    return jnp.concatenate(ranks, axis=1).astype(jnp.int32)


def selection(ranks, row_first, rows):
    wanted = lax.broadcasted_iota(jnp.int32, (rows, ranks.shape[1]), 0) + row_first
    return jnp.where(wanted == ranks, 1.0, 0.0).astype(jnp.bfloat16)


def pack_kernel(plan, step, chunks, ids_ref, slot_ref, chosen_ref, keys_ref, values_ref, *rest):
    outs, (key_rows, value_rows, sems) = rest[: -3], rest[-3:]
    store, core = lax.axis_index("store"), lax.axis_index("sub")
    dest = plan.partner(store, step)
    places, owners, turns, live = find_spans(plan, ids_ref, slot_ref, store, dest)
    copies = []
    for rank in range(plan.capacity):
        rows = pl.ds(rank * plan.half, plan.half)
        copies.append(pltpu.make_async_copy(keys_ref.at[places[rank]], key_rows.at[rows], sems.at[0, rank]))
        copies.append(pltpu.make_async_copy(values_ref.at[places[rank]], value_rows.at[rows], sems.at[1, rank]))
    for copy in copies:
        copy.start()
    ranks = live_ranks(plan, chosen_ref, dest, core, owners, turns, live)
    for copy in copies:
        copy.wait()
    for row_first, rows in [tile for chunk in chunks for tile in tiles(*chunk)]:
        first = row_first // plan.half * plan.half
        select = selection(ranks[:, first:], row_first, rows)
        for turn in range(plan.cores):
            start = plan.kv_start(lax.rem(core + turn, plan.cores))
            for number, (chunk_first, chunk_rows) in enumerate(chunks):
                if chunk_first <= row_first < chunk_first + chunk_rows:
                    out = outs[number * plan.cores + turn]
                    place = slice(row_first - chunk_first, row_first - chunk_first + rows)
            for source, offset in ((key_rows, 0), (value_rows, plan.width)):
                out[place, offset : offset + plan.width] = jnp.dot(
                    select, source[first:, pl.ds(start, plan.width)], preferred_element_type=jnp.float32
                ).astype(jnp.bfloat16)


def tiles(start, rows, size=256):
    return [(start + first, min(size, rows - first)) for first in range(0, rows, size)]


def pack(plan, step, chunks, ids, slots, chosen, store_keys, store_values):
    shapes = [
        pltpu.HBM((rows, 2 * plan.width), jnp.bfloat16)
        for _, rows in chunks
        for _ in range(plan.cores)
    ]
    return pl.pallas_call(
        functools.partial(pack_kernel, plan, step, chunks),
        out_shape=shapes,
        grid_spec=pltpu.PrefetchScalarGridSpec(
            num_scalar_prefetch=2,
            grid=(1,),
            in_specs=[
                pl.BlockSpec(chosen.shape, lambda i, *_: (0, 0)),
                pl.BlockSpec(memory_space=pl.ANY),
                pl.BlockSpec(memory_space=pl.ANY),
            ],
            out_specs=[pl.BlockSpec(s.shape, lambda i, *_: (0, 0)) for s in shapes],
            scratch_shapes=[
                pltpu.VMEM((plan.source_rows, plan.kv_columns), jnp.bfloat16),
                pltpu.VMEM((plan.source_rows, plan.kv_columns), jnp.bfloat16),
                pltpu.SemaphoreType.DMA((2, plan.capacity)),
            ],
        ),
        cost_estimate=pl.CostEstimate(
            flops=4 * plan.source_rows**2 * plan.kv_columns,
            bytes_accessed=8 * plan.source_rows * plan.kv_columns,
            transcendentals=0,
        ),
    )(ids, slots, chosen, store_keys, store_values)


def spans_before(position_row, start):
    return jnp.sum(jnp.where(position_row < start, 1.0, 0.0), axis=1, keepdims=True)


def blend(plan, stage, table, left_ref, my_pos_ref, fresh_key_ref, fresh_value_ref, joined, keys, values):
    core = lax.axis_index("sub")
    held = sum(rows for _, rows in stage.chunks)
    rows = min(plan.half + 16, held)

    def one_turn(turn, unused):
        source_core = lax.rem(core + plan.cores - turn, plan.cores)

        def one_rank(rank, offset):
            owner, base = table[2 * rank], table[2 * rank + 1] + source_core * plan.half
            live = owner >= 0
            request = jnp.maximum(owner, 0)
            listed = my_pos_ref[pl.ds(request, 1), :]
            first = spans_before(listed, base)
            taken = spans_before(listed, base + plan.half) - first

            @pl.when(live & (rank >= stage.ranks[0]))
            def _():
                token = lax.broadcasted_iota(jnp.int32, (plan.half, SEL), 0) + base
                same = jnp.where(listed == token, 1.0, 0.0)
                ahead = jnp.sum(jnp.where(listed < token, 1.0, 0.0), axis=1, keepdims=True)
                chosen = jnp.sum(same, axis=1, keepdims=True)
                row = lax.broadcasted_iota(jnp.int32, (plan.half, 1), 0).astype(jnp.float32)
                row = row + offset - ahead + first
                row = jnp.where(chosen > 0.5, -1.0, row).astype(jnp.int32)
                fresh_pick = same.astype(jnp.bfloat16)
                key = jnp.dot(fresh_pick, fresh_key_ref[request, :SEL, :], preferred_element_type=jnp.float32)
                value = jnp.dot(fresh_pick, fresh_value_ref[request, :SEL, :], preferred_element_type=jnp.float32)
                below = jnp.max(offset.astype(jnp.int32)) // 16 * 16
                below = pl.multiple_of(jnp.minimum(below, held - rows), 16)
                lane = lax.broadcasted_iota(jnp.int32, (plan.half, rows), 1) + below
                pick = jnp.where(lane == row, 1.0, 0.0).astype(jnp.bfloat16)
                both = jnp.dot(pick, joined[turn, pl.ds(below, rows), :], preferred_element_type=jnp.float32)
                at = rank - stage.ranks[0]
                place = pl.ds(pl.multiple_of(source_core * plan.half, plan.half), plan.half)
                keys[at, place, :] = (key + both[:, : plan.width]).astype(jnp.bfloat16)
                values[at, place, :] = (value + both[:, plan.width :]).astype(jnp.bfloat16)
                if stage.left:
                    @pl.when(left_ref[0] > 0)
                    def _():
                        over = lax.broadcasted_iota(jnp.int32, (plan.half, plan.left_rows), 1) + plan.sent_rows
                        extra = jnp.where(over == row, 1.0, 0.0).astype(jnp.bfloat16)
                        more = jnp.dot(extra, joined[turn, held:, :], preferred_element_type=jnp.float32)
                        more = more.astype(jnp.bfloat16)
                        keys[at, place, :] += more[:, : plan.width]
                        values[at, place, :] += more[:, plan.width :]

            return offset + (plan.half - taken) * live.astype(jnp.float32)

        lax.fori_loop(0, stage.ranks[-1] + 1, one_rank, jnp.zeros((1, 1), jnp.float32))
        return unused

    lax.fori_loop(0, plan.cores, one_turn, 0)


def attend_kernel(plan, stage, *refs):
    refs = list(refs)

    def take(count):
        taken = refs[:count]
        del refs[:count]
        return taken

    ids_ref, slot_ref, pos_ref, len_ref, _, left_ref = take(6)
    column_ref, my_pos_ref, fresh_key_ref, fresh_value_ref = take(4)
    if stage.opening:
        (query_in,) = take(1)
    else:
        query, sizes = take(2)
        take(3)
    streams = take((len(stage.chunks) + stage.left) * plan.cores)
    if stage.closing:
        (out_ref,) = take(1)
    total_ref, sums_ref, top_ref = take(3)
    if stage.opening:
        query, sizes = take(2)
    keys, values, joined, table, arrivals = take(5)
    request = pl.program_id(0)
    store = lax.axis_index("store")
    span = plan.half * plan.cores
    last = ROWS // TILE
    bunch = plan.per_kv * TILE

    @pl.when(request == 0)
    def _():
        copies, at = [], 0
        for number, (_, rows) in enumerate(stage.pieces(plan)):
            for turn in range(plan.cores):
                index = number * plan.cores + turn
                source = streams[index]
                if number == len(stage.chunks):
                    source = source.at[pl.ds(stage.left_at(plan, turn), rows)]
                copies.append(
                    pltpu.make_async_copy(source, joined.at[turn, pl.ds(at, rows)], arrivals.at[index])
                )
            at += rows
        for copy in copies:
            copy.start()
        source = plan.origin(store, stage.step)
        _, owners, turns, live = find_spans(plan, ids_ref, slot_ref, source, store)
        for rank in range(plan.capacity):
            table[2 * rank] = jnp.where(live[rank] > 0, owners[rank], -1)
            table[2 * rank + 1] = turns[rank] * SPAN
        for copy in copies:
            copy.wait()
        blend(plan, stage, table, left_ref, my_pos_ref, fresh_key_ref, fresh_value_ref, joined, keys, values)

    def rows_of(tile):
        return pl.ds(pl.multiple_of(tile * TILE, 16), TILE)

    def bunch_of(tile, count=1):
        return pl.ds(pl.multiple_of(tile * bunch, 16), count * bunch)

    def members():
        for kv in range(plan.kv_used):
            for member in range(plan.per_kv):
                head = kv * plan.per_kv + member
                yield kv, member, slice(head * HD, (head + 1) * HD)

    if stage.opening:
        def prepare(tile, most):
            long, low = most
            for kv, member, lanes in members():
                place = pl.ds(pl.multiple_of(tile * bunch + member * TILE, 16), TILE)
                taken = query_in[0, rows_of(tile), lanes]
                query[request, kv, place, :] = taken
                taken = taken.astype(jnp.float32)
                own = fresh_key_ref[request, rows_of(tile), kv * HD : (kv + 1) * HD].astype(jnp.float32)
                product = jnp.broadcast_to(jnp.sum(taken * own, axis=1, keepdims=True), (TILE, HD))
                top_ref[request, kv, place, :] = product
                total_ref[request, kv, place, :] = jnp.zeros((TILE, HD), jnp.float32)
                sums_ref[request, kv, place, :] = jnp.zeros((TILE, HD), jnp.float32)
                long = jnp.maximum(long, jnp.sum(jnp.abs(taken), axis=1, keepdims=True))
                low = jnp.maximum(low, -product)
            return long, low

        none = jnp.zeros((TILE, HD), jnp.float32)
        long, low = lax.fori_loop(0, last, prepare, (none, none))
        sizes[request, 0] = long
        sizes[request, 1] = low

    def masks(tile, count, width, base):
        lane = lax.broadcasted_iota(jnp.int32, (TILE, width), 1) + base
        return [lane <= column_ref[0, rows_of(tile + more), :] for more in range(count)]

    def quick(tile, count, kv, key, extended, allowed):
        rows = bunch_of(tile, count)
        scores = lax.dot_general(
            query[request, kv, rows, :], key, (((1,), (1,)), ((), ())), preferred_element_type=jnp.float32
        )
        width = key.shape[0] // HD
        powers = []
        for more in range(count):
            for member in range(plan.per_kv):
                first = more * bunch + member * TILE
                place = pl.ds(pl.multiple_of(tile * bunch + first, 16), TILE)
                shift = jnp.concatenate([top_ref[request, kv, place, :]] * width, axis=1)
                power = jnp.exp2((scores[first : first + TILE] - shift) * LOG_SCALE)
                powers.append(jnp.where(allowed[more], power, 0.0).astype(jnp.bfloat16))
        update = jnp.dot(jnp.concatenate(powers, axis=0), extended, preferred_element_type=jnp.float32)
        total_ref[request, kv, rows, :] += update[:, :HD]
        sums_ref[request, kv, rows, :] += update[:, HD:]

    def careful(tile, count, kv, key, extended, allowed):
        def one(number, unused):
            place = pl.ds(pl.multiple_of(tile * bunch + number * TILE, 16), TILE)
            scores = lax.dot_general(
                query[request, kv, place, :], key, (((1,), (1,)), ((), ())), preferred_element_type=jnp.float32
            )
            scores = jnp.where(allowed[0], scores, NEGATIVE)
            old_top = top_ref[request, kv, place, :]
            new_top = jnp.maximum(old_top, jnp.max(scores, axis=1, keepdims=True))
            shift = jnp.concatenate([new_top] * (key.shape[0] // HD), axis=1)
            powers = jnp.exp2((scores - shift) * LOG_SCALE)
            update = jnp.dot(powers.astype(jnp.bfloat16), extended, preferred_element_type=jnp.float32)
            factor = jnp.exp2((old_top - new_top) * LOG_SCALE)
            total_ref[request, kv, place, :] = total_ref[request, kv, place, :] * factor + update[:, :HD]
            sums_ref[request, kv, place, :] = sums_ref[request, kv, place, :] * factor + update[:, HD:]
            top_ref[request, kv, place, :] = new_top
            return unused

        lax.fori_loop(0, plan.per_kv, one, 0)

    def extend(value):
        return jnp.concatenate([value, jnp.ones(value.shape, jnp.bfloat16)], axis=1)

    def last_pos(tile):
        return pos_ref[request * ROWS + (tile + 1) * TILE - 1]

    def run(act, pairs):
        def span_tiles(at, base, tile, count):
            allowed = masks(tile, count, span, base)
            for kv in range(plan.kv_used):
                lanes = slice(kv * HD, (kv + 1) * HD)
                act(tile, count, kv, keys[at, :, lanes], extend(values[at, :, lanes]), allowed)

        def one_span(at, unused):
            rank = at + stage.ranks[0]
            owner, base = table[2 * rank], table[2 * rank + 1]

            @pl.when(owner == request)
            def _():
                if not pairs:
                    def step(tile, unused):
                        span_tiles(at, base, tile, 1)
                        return unused

                    lax.fori_loop(0, last, step, 0)
                    return

                @pl.when(last_pos(0) >= base)
                def _():
                    span_tiles(at, base, 0, 1)

                first = jnp.int32(0)
                for pair in range(last // 2):
                    first = first + (last_pos(2 * pair + 2) < base).astype(jnp.int32)

                def step(pair, unused):
                    span_tiles(at, base, 2 * pair + 1, 2)
                    return unused

                lax.fori_loop(first, last // 2, step, 0)

            return unused

        lax.fori_loop(0, len(stage.ranks), one_span, 0)
        if stage.opening:
            def ask(tile, unused):
                allowed = masks(tile, 1, 2 * QLEN, CTX)
                for kv in range(plan.kv_used):
                    lanes = slice(kv * HD, (kv + 1) * HD)
                    key, value = fresh_key_ref[request, SEL:, lanes], fresh_value_ref[request, SEL:, lanes]
                    key = jnp.concatenate([key, jnp.zeros_like(key)], axis=0)
                    value = jnp.concatenate([value, jnp.zeros_like(value)], axis=0)
                    act(tile, 1, kv, key, extend(value), allowed)
                return unused

            lax.fori_loop(SEL // TILE, last, ask, 0)

    greatest = jnp.max(jnp.abs(keys[...].astype(jnp.float32)))
    if stage.opening:
        greatest = jnp.maximum(greatest, jnp.max(jnp.abs(fresh_key_ref[request].astype(jnp.float32))))
    reach = (greatest * jnp.max(sizes[request, 0]) + jnp.max(sizes[request, 1])) * LOG_SCALE
    held = reach < LIMIT

    @pl.when(held)
    def _():
        run(quick, True)

    @pl.when(jnp.logical_not(held))
    def _():
        run(careful, False)

    if stage.closing:
        def finish(tile, unused):
            row = lax.broadcasted_iota(jnp.int32, (TILE, HD), 0) + tile * TILE
            live = row < SEL + len_ref[request]
            for kv, member, lanes in members():
                place = pl.ds(pl.multiple_of(tile * bunch + member * TILE, 16), TILE)
                result = total_ref[request, kv, place, :] / sums_ref[request, kv, place, :]
                out_ref[0, rows_of(tile), lanes] = jnp.where(live, result, 0.0).astype(jnp.bfloat16)
            return unused

        lax.fori_loop(0, last, finish, 0)


def attend(plan, stage, state, arrays, fresh, ids, slots, my_pos, pos, pos_column, lengths, left_over):
    fresh_query, fresh_keys, fresh_values = fresh
    req_dev = plan.req_dev
    row_block = lambda width: pl.BlockSpec((1, ROWS, width), lambda r, *_: (r, 0, 0))
    whole = lambda array: pl.BlockSpec(array.shape, lambda r, *_: (0,) * array.ndim)
    kept = pl.BlockSpec(memory_space=pltpu.VMEM)
    fresh_block = pl.BlockSpec((req_dev, ROWS, plan.width), lambda r, *s: (0, 0, s[4][0]))
    kv_block = jnp.reshape(plan.kv_block, (1,))
    operands = [ids, slots, pos, lengths, kv_block, left_over, pos_column, my_pos, fresh_keys, fresh_values]
    specs = [row_block(1), whole(my_pos), fresh_block, fresh_block]
    aliases = {}
    stacked = (req_dev, plan.kv_used, plan.q_heads // plan.kv_used * ROWS, HD)
    out_shape, out_specs = [], []
    if stage.closing:
        out_shape = [jax.ShapeDtypeStruct(fresh_query.shape, jnp.bfloat16)]
        out_specs = [row_block(plan.q_columns)]
    if stage.opening:
        operands.append(fresh_query)
        specs.append(row_block(plan.q_columns))
    else:
        aliases = {len(operands) + 2 + i: len(out_shape) + i for i in range(3)}
        operands += [state[3], state[4], *state[:3]]
        specs += [kept] * 5
    joined_rows = sum(rows for _, rows in stage.pieces(plan))
    if stage.opening:
        arrays = [pltpu.with_memory_space_constraint(array, pltpu.HBM) for array in arrays]
    operands += arrays
    specs += [pl.BlockSpec(memory_space=pltpu.HBM if stage.opening else pl.ANY)] * len(arrays)
    span = plan.half * plan.cores
    scratch = [pltpu.VMEM((len(stage.ranks), span, plan.width), jnp.bfloat16)] * 2
    scratch += [pltpu.VMEM((plan.cores, joined_rows, 2 * plan.width), jnp.bfloat16)]
    scratch += [pltpu.SMEM((2 * plan.capacity,), jnp.int32), pltpu.SemaphoreType.DMA((len(arrays),))]
    out_shape += [pltpu.VMEM(stacked, jnp.float32)] * 3
    out_specs += [kept] * 3
    if stage.opening:
        out_shape += [pltpu.VMEM(stacked, jnp.bfloat16), pltpu.VMEM((req_dev, 2, TILE, HD), jnp.float32)]
        out_specs += [kept] * 2
    scores = len(stage.ranks) * span * ROWS * plan.q_heads
    result = pl.pallas_call(
        functools.partial(attend_kernel, plan, stage),
        out_shape=out_shape,
        grid_spec=pltpu.PrefetchScalarGridSpec(
            num_scalar_prefetch=6,
            grid=(req_dev,),
            in_specs=specs,
            out_specs=out_specs,
            scratch_shapes=scratch,
        ),
        input_output_aliases=aliases,
        compiler_params=pltpu.CompilerParams(vmem_limit_bytes=20 << 20),
        cost_estimate=pl.CostEstimate(
            flops=4 * scores * HD,
            bytes_accessed=req_dev * ROWS * plan.q_columns * 4,
            transcendentals=scores,
        ),
    )(*operands)
    if stage.closing:
        return result[0]
    return result if stage.opening else list(result) + list(state[3:])


class Stage:
    def __init__(self, step, ranks, chunks, left):
        self.step, self.ranks, self.chunks, self.left = step, ranks, chunks, left
        self.opening = self.closing = False

    def pieces(self, plan):
        return self.chunks + [(plan.sent_rows, plan.left_rows)] * self.left

    def left_at(self, plan, turn):
        return ((self.step - 1) * plan.cores + turn) * plan.left_rows


def most_live(plan, span_ids, span_slot, select_pos):
    halves = CTX // plan.half
    listed = (select_pos // plan.half)[:, :, None] == jnp.arange(halves, dtype=jnp.int32)
    live = plan.half - jnp.sum(listed.astype(jnp.int32), axis=1)
    spans = span_ids.reshape(plan.stores, plan.refs)
    known = spans[:, :, None] == jnp.arange(span_slot.shape[0], dtype=jnp.int32)
    owner = jnp.sum(jnp.where(known, span_slot // plan.ch_dev, 0), axis=2)
    live = live.reshape(plan.stores, plan.refs, plan.cores)
    theirs = owner[:, :, None] == jnp.arange(plan.stores, dtype=jnp.int32)
    counts = jnp.sum(jnp.where(theirs[..., None], live[:, :, None, :], 0), axis=1)
    most = jnp.max(counts).reshape(1)
    groups = lax.axis_size("groups")
    others = [
        lax.ppermute(most, "groups", [(g, (g + turn) % groups) for g in range(groups)])
        for turn in range(1, groups)
    ]
    for other in others:
        most = jnp.maximum(most, other)
    return most


def body(
    fresh_query,
    fresh_keys,
    fresh_values,
    store_keys,
    store_values,
    span_ids,
    span_slot,
    select_pos,
    ask_len,
):
    plan = Plan(fresh_query, store_keys, span_ids)
    store_index = lax.axis_index("store")
    ids = span_ids.reshape(-1)
    chosen = jnp.transpose(select_pos)
    steps = list(range(1, plan.stores))
    arrived = {}
    for step in steps + [0]:
        chunks = plan.chunks(step)
        own_ids = ids
        if step != steps[0]:
            own_ids, _ = lax.optimization_barrier((ids, before))
        packed = pack(plan, step, chunks, own_ids, span_slot, chosen, store_keys, store_values)
        before = packed[0]
        at = 0
        for chunk in range(len(chunks)):
            for turn in range(plan.cores):
                block = packed[at]
                at += 1
                if step != 0 or turn != 0:
                    block = lax.ppermute(block, ("store", "sub"), plan.pairs(step, turn))
                arrived[(step, chunk, turn)] = block
    left, left_over = [], jnp.zeros((1,), jnp.int32)
    if plan.left_rows:
        most = most_live(plan, span_ids, span_slot, select_pos)
        left_over = (most > plan.sent_rows).astype(jnp.int32)

        def send_left():
            blocks = []
            for step in steps:
                rest = pack(
                    plan, step, [(plan.sent_rows, plan.left_rows)], ids, span_slot, chosen, store_keys, store_values
                )
                for turn in range(plan.cores):
                    blocks.append(lax.ppermute(rest[turn], ("store", "sub"), plan.pairs(step, turn)))
            return jnp.concatenate(blocks, axis=0)

        def nothing():
            return jnp.zeros((len(steps) * plan.cores * plan.left_rows, 2 * plan.width), jnp.bfloat16)

        blocks = lax.cond(left_over[0] > 0, send_left, nothing)
        left = [blocks] * plan.cores
    my_pos = lax.dynamic_slice_in_dim(select_pos, store_index * plan.req_dev, plan.req_dev, 0)
    lengths = lax.dynamic_slice_in_dim(ask_len, store_index * plan.req_dev, plan.req_dev, 0)
    asked = jnp.broadcast_to(CTX + jnp.arange(QLEN, dtype=jnp.int32), (plan.req_dev, QLEN))
    pos = jnp.concatenate([my_pos, asked], axis=1)
    pos_column = pos[:, :, None]
    pos = pos.reshape(-1)
    all_ranks = list(range(plan.capacity))
    stages = []
    for step in [0] + steps:
        chunks = plan.chunks(step)
        groups = [all_ranks]
        if len(chunks) == plan.capacity:
            groups = [[rank] for rank in all_ranks]
        elif len(chunks) == 2:
            groups = [all_ranks[:-1], all_ranks[-1:]]
        for number, ranks in enumerate(groups):
            remains = step != 0 and plan.left_rows > 0 and ranks[-1] == all_ranks[-1]
            stages.append(Stage(step, ranks, chunks[: number + 1], int(remains)))
    if len(stages) > plan.stores and len(plan.chunks(steps[-1])) == plan.capacity:
        late = len(stages) - plan.capacity
        stages[late - 1], stages[late] = stages[late], stages[late - 1]
    stages[0].opening = True
    stages[-1].closing = True
    state = None
    for stage in stages:
        arrays = [
            arrived[(stage.step, chunk, turn)]
            for chunk in range(len(stage.chunks))
            for turn in range(plan.cores)
        ]
        if stage.left:
            arrays = arrays + left
        state = attend(
            plan, stage, state, arrays, (fresh_query, fresh_keys, fresh_values), ids, span_slot,
            my_pos, pos, pos_column, lengths, left_over,
        )
    return state


def solution(mesh):
    placed = (
        P(("groups", "store"), None, ("head", "sub")),
        P(("groups", "store"), None, "head"),
        P(("groups", "store"), None, "head"),
        P(("groups", "store"), "sub", "head"),
        P(("groups", "store"), "sub", "head"),
        P("groups", None),
        P("groups"),
        P("groups", None),
        P("groups"),
    )
    return jax.shard_map(
        body,
        mesh=mesh,
        in_specs=placed,
        out_specs=P(("groups", "store"), None, ("head", "sub")),
        check_vma=False,
    )
```
